32 devices in a mesh: seq: 16 (over z, x, core), wshard: 2 (over y).
Axes of the slice: x: 2, y: 2, z: 4, core: 2. Of those that a mesh axis runs over, the one named last changes fastest.
Arguments:
- inputs: bfloat16 [8192, 640], P(('seq', 'wshard')), may hold values from -6 to 6
- doc_ids: int32 [8192], P(('seq', 'wshard')), may hold values from 0 to 2, never falling along the last dimension, each value on 1 to 4096 neighbouring positions
- w_query: bfloat16 [640, 1024], P('wshard'), may hold values from -0.25 to 0.25
- w_key: bfloat16 [640, 256], P('wshard'), may hold values from -0.25 to 0.25
- w_value: bfloat16 [640, 256], P('wshard'), may hold values from -0.25 to 0.25
- w_out: bfloat16 [1024, 640], P('wshard'), may hold values from -0.1875 to 0.1875
- w_gate: bfloat16 [640, 2048], P('wshard'), may hold values from -0.25 to 0.25
- w_up: bfloat16 [640, 2048], P('wshard'), may hold values from -0.25 to 0.25
- w_down: bfloat16 [2048, 640], P('wshard'), may hold values from -0.125 to 0.125
- gain_in: bfloat16 [640], P('wshard'), may hold values from -0.5 to 1
- gain_attn_post: bfloat16 [640], P('wshard'), may hold values from -0.5 to 1
- gain_ff_pre: bfloat16 [640], P('wshard'), may hold values from -0.5 to 1
- gain_ff_post: bfloat16 [640], P('wshard'), may hold values from -0.5 to 1
- gain_query: bfloat16 [256], P('wshard'), may hold values from -0.5 to 1
- gain_key: bfloat16 [256], P('wshard'), may hold values from -0.5 to 1
- cotangent: bfloat16 [8192, 640], P(('seq', 'wshard')), may hold values from -6 to 6
Outputs:
- layer_out: bfloat16 [8192, 640], P(('seq', 'wshard'))
- grad_inputs: float32 [8192, 640], P(('seq', 'wshard'))
- grad_w_query: float32 [640, 1024], P('wshard')
- grad_w_key: float32 [640, 256], P('wshard')
- grad_w_value: float32 [640, 256], P('wshard')
- grad_w_out: float32 [1024, 640], P('wshard')
- grad_w_gate: float32 [640, 2048], P('wshard')
- grad_w_up: float32 [640, 2048], P('wshard')
- grad_w_down: float32 [2048, 640], P('wshard')
- grad_gain_in: float32 [640], P('wshard')
- grad_gain_attn_post: float32 [640], P('wshard')
- grad_gain_ff_pre: float32 [640], P('wshard')
- grad_gain_ff_post: float32 [640], P('wshard')
- grad_gain_query: float32 [256], P('wshard')
- grad_gain_key: float32 [256], P('wshard')
The draws below stay inside these ranges and needn't reach their ends.
Inputs may be any that keep to these rules, and one draw needn't show every extreme that they name: `doc_ids`: document numbers never fall along the token stream; every document has 1 to 4096 tokens, one exactly 4096.
All inputs are finite; a program needn't handle non-finite values.
Results may differ from the reference program's by a relative error of at most 0.025.
Values may be sent and summed in bfloat16 or wider, within the bound.
A program may use at most 128 MiB of HBM per device.

```python
import math
import jax
import jax.numpy as jnp
import numpy as np
from jax import lax

D = 640
H = 4
HD = 256
FF = 2048
WINDOW = 512
TOK_DEV = 256
DOCS = 3
TOKENS = 8192
MOST_DOC = 4096
N_SEQ = 16
N_WSHARD = 2


def block_scale(own_key, extent, shards, least, high):
    level, own = 1.0, jax.random.fold_in(own_key, 6)
    for axis_at, shards_of in shards:
        steps = jnp.exp(jax.random.uniform(jax.random.fold_in(own, axis_at), (shards_of,), jnp.float32, least / len(shards), high / len(shards)))
        level = level * jnp.repeat(steps, extent[axis_at] // shards_of).reshape([-1 if axis == axis_at else 1 for axis in range(len(extent))])
    return level


def profile(number_of, total, reach, lean):
    portions = [(1 << 20) // math.isqrt(rank ** lean) + 1 for rank in range(2, number_of + 1)]
    spare, holding = total - reach - (number_of - 1), [1] * (number_of - 1)
    while spare > 0:
        movable = [i for i in range(number_of - 1) if holding[i] < reach]
        mass, budget = sum([portions[i] for i in movable]), spare
        for i in movable:
            addition = min(reach - holding[i], max(1, budget * portions[i] // mass), spare)
            holding[i] = holding[i] + addition
            spare = spare - addition
    return np.array([reach] + holding)


def ragged_sizes(own_key, number_of, total, reach, slope):
    if number_of == 2:
        one = jax.random.randint(own_key, (), max(1, total - reach), min(reach, total - 1) + 1)
        return jnp.stack([one, total - one])
    sizes = jnp.asarray(profile(number_of, total, reach, slope), jnp.int32)
    twos = (number_of - 1) // 2
    donor, taker = sizes[1:1 + 2 * twos:2], sizes[2:2 + 2 * twos:2]
    slack = jnp.minimum(donor - 1, reach - taker)
    passed = jax.random.randint(jax.random.fold_in(own_key, 1), (twos,), 0, 1 << 20) % (slack + 1)
    sizes = sizes.at[1:1 + 2 * twos:2].set(donor - passed).at[2:2 + 2 * twos:2].set(taker + passed)
    return sizes[jax.random.permutation(jax.random.fold_in(own_key, 2), number_of)]


def noise(own_key, extent, scale, limit, cuts=(), kind=jnp.bfloat16):
    values = jax.random.normal(own_key, extent, jnp.float32) * scale
    if len(cuts) > 0:
        values = block_scale(own_key, extent, cuts, -0.22, 0.18) * values
    return jnp.clip(values, min=-limit, max=limit).astype(kind)


def setup_inputs(seed: int = 0) -> dict:
    streams_of = jax.random.split(jax.random.key(seed), 17)
    return {
        "inputs": noise(streams_of[0], (TOKENS, D), 1.0, 6.0, ((0, 32),)),
        "doc_ids": jnp.searchsorted(jnp.cumsum(ragged_sizes(streams_of[1], DOCS, TOKENS, MOST_DOC, 0)), jnp.arange(TOKENS), side="right").astype(jnp.int32),
        "w_query": noise(streams_of[2], (D, H * HD), D ** -0.5, 0.25, ((0, 2),)),
        "w_key": noise(streams_of[3], (D, HD), D ** -0.5, 0.25, ((0, 2),)),
        "w_value": noise(streams_of[4], (D, HD), D ** -0.5, 0.25, ((0, 2),)),
        "w_out": noise(streams_of[5], (H * HD, D), (H * HD) ** -0.5, 0.1875, ((0, 2),)),
        "w_gate": noise(streams_of[6], (D, FF), D ** -0.5, 0.25, ((0, 2),)),
        "w_up": noise(streams_of[7], (D, FF), D ** -0.5, 0.25, ((0, 2),)),
        "w_down": noise(streams_of[8], (FF, D), FF ** -0.5, 0.125, ((0, 2),)),
        "gain_in": jnp.clip(-0.5 + 1.5 * jax.random.uniform(streams_of[9], (D,), jnp.float32) ** block_scale(streams_of[9], (D,), ((0, 2),), -0.2, 0.2), -0.5, 1.0).astype(jnp.bfloat16),
        "gain_attn_post": jnp.clip(-0.5 + 1.5 * jax.random.uniform(streams_of[10], (D,), jnp.float32) ** block_scale(streams_of[10], (D,), ((0, 2),), -0.2, 0.2), -0.5, 1.0).astype(jnp.bfloat16),
        "gain_ff_pre": jnp.clip(-0.5 + 1.5 * jax.random.uniform(streams_of[11], (D,), jnp.float32) ** block_scale(streams_of[11], (D,), ((0, 2),), -0.2, 0.2), -0.5, 1.0).astype(jnp.bfloat16),
        "gain_ff_post": jnp.clip(-0.5 + 1.5 * jax.random.uniform(streams_of[12], (D,), jnp.float32) ** block_scale(streams_of[12], (D,), ((0, 2),), -0.2, 0.2), -0.5, 1.0).astype(jnp.bfloat16),
        "gain_query": jnp.clip(-0.5 + 1.5 * jax.random.uniform(streams_of[13], (HD,), jnp.float32) ** block_scale(streams_of[13], (HD,), ((0, 2),), -0.2, 0.2), -0.5, 1.0).astype(jnp.bfloat16),
        "gain_key": jnp.clip(-0.5 + 1.5 * jax.random.uniform(streams_of[14], (HD,), jnp.float32) ** block_scale(streams_of[14], (HD,), ((0, 2),), -0.2, 0.2), -0.5, 1.0).astype(jnp.bfloat16),
        "cotangent": noise(streams_of[15], (TOKENS, D), 1.0, 6.0, ((0, 32),)),
    }


NORM_EPSILON = 1e-06
ROPE_BASE = 10000.0
MASK_FLOOR = -1e+30

def rms_gain(tensor, gain_vec):
    factor = lax.rsqrt(lax.optimization_barrier(jnp.mean(tensor * tensor, axis=-1, keepdims=True)) + NORM_EPSILON)
    return tensor * factor * (1.0 + gain_vec)

def rope_tables(positions, head_width):
    half_width = head_width // 2
    exponent = jnp.arange(half_width, dtype=jnp.float32) * (2.0 / head_width)
    inverse = jnp.exp(-jnp.log(ROPE_BASE) * exponent)
    angles = positions.astype(jnp.float32)[:, None] * inverse[None, :]
    return (jnp.cos(angles), jnp.sin(angles))

def norm_rope(tensor, gain_vec, cos_table, sin_table):
    normed = rms_gain(tensor, gain_vec)
    half_width = tensor.shape[-1] // 2
    front_part = normed[..., :half_width]
    back_part = normed[..., half_width:]
    cos_rows = cos_table[:, None, :]
    sin_rows = sin_table[:, None, :]
    return jnp.concatenate([front_part * cos_rows - back_part * sin_rows, back_part * cos_rows + front_part * sin_rows], axis=-1)

def geglu(gate_pre, up_pre):
    return jax.nn.gelu(gate_pre, approximate=True) * up_pre

def window_mask(query_pos, key_pos, query_doc, key_doc):
    distance = query_pos[:, None] - key_pos[None, :]
    return (distance >= 0) & (distance < WINDOW) & (key_pos[None, :] >= 0) & (query_doc[:, None] == key_doc[None, :])

def log_totals(scores, allowed):
    row_peak = lax.optimization_barrier(jnp.max(scores, axis=-1, keepdims=True))
    row_total = lax.optimization_barrier(jnp.sum(jnp.where(allowed[None], jnp.exp(scores - row_peak), 0.0), axis=-1, keepdims=True))
    return row_peak + jnp.log(row_total)

def round_bf16(tensor):
    return lax.optimization_barrier(tensor.astype(jnp.bfloat16)).astype(jnp.float32)

def device_gain(per_row):
    device_count = N_SEQ * N_WSHARD
    parts = lax.optimization_barrier(jnp.sum(per_row.reshape(device_count, -1, per_row.shape[-1]), axis=1))
    return lax.optimization_barrier(jnp.sum(round_bf16(parts), axis=0))

def rms_pull(tensor, gain_vec, grad_out):
    _, pullback = jax.vjp(rms_gain, tensor, jnp.broadcast_to(gain_vec, tensor.shape))
    grad_tensor, grad_gain_rows = pullback(grad_out)
    return (grad_tensor, device_gain(grad_gain_rows))

def reference(inputs, doc_ids, w_query, w_key, w_value, w_out, w_gate, w_up, w_down, gain_in, gain_attn_post, gain_ff_pre, gain_ff_post, gain_query, gain_key, cotangent):
    token_count = inputs.shape[0]
    block_count = token_count // WINDOW
    device_count = N_SEQ * N_WSHARD
    score_scale = HD ** (-0.5)
    in_gain = gain_in.astype(jnp.float32)
    attn_post_gain = gain_attn_post.astype(jnp.float32)
    ff_pre_gain = gain_ff_pre.astype(jnp.float32)
    ff_post_gain = gain_ff_post.astype(jnp.float32)
    query_gain = gain_query.astype(jnp.float32)
    key_gain = gain_key.astype(jnp.float32)
    x_float = inputs.astype(jnp.float32)
    positions = jnp.arange(token_count, dtype=jnp.int32)
    cos_table, sin_table = rope_tables(positions, HD)
    normed_in = rms_gain(x_float, in_gain).astype(jnp.bfloat16)
    query_raw = jnp.dot(normed_in, w_query, preferred_element_type=jnp.float32).reshape(token_count, H, HD)
    key_raw = jnp.dot(normed_in, w_key, preferred_element_type=jnp.float32)[:, None, :]
    values = jnp.dot(normed_in, w_value, preferred_element_type=jnp.float32).astype(jnp.bfloat16)
    queries = norm_rope(query_raw, query_gain, cos_table, sin_table).astype(jnp.bfloat16)
    key_rot = norm_rope(key_raw, key_gain, cos_table, sin_table)[:, 0].astype(jnp.bfloat16)
    key_pad = jnp.concatenate([jnp.zeros((WINDOW, HD), jnp.bfloat16), key_rot], 0)
    value_pad = jnp.concatenate([jnp.zeros((WINDOW, HD), jnp.bfloat16), values], 0)
    doc_pad = jnp.concatenate([jnp.zeros((WINDOW,), jnp.int32), doc_ids], 0)

    def block_view(block_index):
        first_row = (block_index * WINDOW).astype(jnp.int32)
        block_queries = lax.dynamic_slice_in_dim(queries, first_row, WINDOW, 0)
        block_keys = lax.dynamic_slice_in_dim(key_pad, first_row, 2 * WINDOW, 0)
        block_values = lax.dynamic_slice_in_dim(value_pad, first_row, 2 * WINDOW, 0)
        query_pos = first_row + jnp.arange(WINDOW, dtype=jnp.int32)
        key_pos = first_row - WINDOW + jnp.arange(2 * WINDOW, dtype=jnp.int32)
        query_doc = lax.dynamic_slice_in_dim(doc_ids, first_row, WINDOW, 0)
        key_doc = lax.dynamic_slice_in_dim(doc_pad, first_row, 2 * WINDOW, 0)
        allowed = window_mask(query_pos, key_pos, query_doc, key_doc)
        scores = jnp.einsum('qhd,kd->hqk', block_queries.astype(jnp.float32), block_keys.astype(jnp.float32)) * score_scale
        scores = jnp.where(allowed[None], scores, MASK_FLOOR)
        return (block_queries, block_keys, block_values, allowed, scores)

    def forward_block(block_index):
        block_queries, block_keys, block_values, allowed, scores = block_view(block_index)
        log_total = log_totals(scores, allowed)
        soft = round_bf16(jnp.where(allowed[None], jnp.exp(scores - log_total), 0.0))
        mixed = jnp.einsum('hqk,kd->qhd', soft, block_values.astype(jnp.float32))
        return (mixed.reshape(WINDOW, H * HD).astype(jnp.bfloat16), log_total)
    block_ids = jnp.arange(block_count, dtype=jnp.int32)
    attn_blocks, log_blocks = lax.map(forward_block, block_ids)
    attended = attn_blocks.reshape(token_count, H * HD)
    attn_proj = jnp.dot(attended, w_out, preferred_element_type=jnp.float32)
    resid = x_float + rms_gain(attn_proj, attn_post_gain)
    normed_ff = rms_gain(resid, ff_pre_gain).astype(jnp.bfloat16)
    gate_pre = jnp.dot(normed_ff, w_gate, preferred_element_type=jnp.float32)
    up_pre = jnp.dot(normed_ff, w_up, preferred_element_type=jnp.float32)
    hidden = geglu(gate_pre, up_pre).astype(jnp.bfloat16)
    ff_proj = jnp.dot(hidden, w_down, preferred_element_type=jnp.float32)
    layer_out = (resid + rms_gain(ff_proj, ff_post_gain)).astype(jnp.bfloat16)
    grad_top = cotangent.astype(jnp.float32)
    grad_ff_proj, grad_gain_ff_post = rms_pull(ff_proj, ff_post_gain, grad_top)
    grad_ff_proj = grad_ff_proj.astype(jnp.bfloat16)
    grad_hidden = jnp.dot(grad_ff_proj, w_down.T, preferred_element_type=jnp.float32)
    _, pullback = jax.vjp(geglu, gate_pre, up_pre)
    grad_gate, grad_up = pullback(grad_hidden)
    grad_gate = grad_gate.astype(jnp.bfloat16)
    grad_up = grad_up.astype(jnp.bfloat16)
    grad_normed_ff = jnp.dot(grad_gate, w_gate.T, preferred_element_type=jnp.float32) + jnp.dot(grad_up, w_up.T, preferred_element_type=jnp.float32)
    grad_resid_part, grad_gain_ff_pre = rms_pull(resid, ff_pre_gain, grad_normed_ff)
    grad_resid = grad_top + grad_resid_part
    grad_attn_proj, grad_gain_attn_post = rms_pull(attn_proj, attn_post_gain, grad_resid)
    grad_attn_proj = grad_attn_proj.astype(jnp.bfloat16)
    grad_attended = jnp.dot(grad_attn_proj, w_out.T, preferred_element_type=jnp.float32).astype(jnp.bfloat16)
    grad_heads = grad_attended.reshape(token_count, H, HD)

    def backward_block(block_index):
        block_queries, block_keys, block_values, allowed, scores = block_view(block_index)
        first_row = (block_index * WINDOW).astype(jnp.int32)
        soft = jnp.where(allowed[None], jnp.exp(scores - log_blocks[block_index]), 0.0)
        block_grad = lax.dynamic_slice_in_dim(grad_heads, first_row, WINDOW, 0).astype(jnp.float32)
        grad_soft = jnp.einsum('qhd,kd->hqk', block_grad, block_values.astype(jnp.float32))
        row_inner = lax.optimization_barrier(jnp.sum(soft * grad_soft, axis=-1, keepdims=True))
        grad_score = round_bf16(soft * (grad_soft - row_inner) * score_scale)
        grad_query = jnp.einsum('hqk,kd->qhd', grad_score, block_keys.astype(jnp.float32))
        grad_key = jnp.einsum('hqk,qhd->kd', grad_score, block_queries.astype(jnp.float32))
        grad_value = jnp.einsum('hqk,qhd->kd', round_bf16(soft), block_grad)
        return (grad_query, grad_key, grad_value)
    grad_q_blocks, grad_k_blocks, grad_v_blocks = lax.map(backward_block, block_ids)
    grad_queries = grad_q_blocks.reshape(token_count, H, HD)
    spill_keys = jnp.concatenate([grad_k_blocks[1:, :WINDOW], jnp.zeros((1, WINDOW, HD), jnp.float32)], 0)
    spill_values = jnp.concatenate([grad_v_blocks[1:, :WINDOW], jnp.zeros((1, WINDOW, HD), jnp.float32)], 0)
    grad_keys = (grad_k_blocks[:, WINDOW:] + spill_keys).reshape(token_count, HD)
    grad_values = (grad_v_blocks[:, WINDOW:] + spill_values).reshape(token_count, HD).astype(jnp.bfloat16)

    def query_path(tensor, gain_full):
        return norm_rope(tensor, gain_full, cos_table, sin_table)
    _, pullback = jax.vjp(query_path, query_raw, jnp.broadcast_to(query_gain, query_raw.shape))
    grad_query_raw, grad_query_gain_rows = pullback(grad_queries)
    grad_gain_query = device_gain(grad_query_gain_rows)
    _, pullback = jax.vjp(query_path, key_raw, jnp.broadcast_to(key_gain, key_raw.shape))
    grad_key_raw, grad_key_gain_rows = pullback(grad_keys[:, None, :])
    grad_gain_key = device_gain(grad_key_gain_rows)
    grad_query_raw = grad_query_raw.reshape(token_count, H * HD).astype(jnp.bfloat16)
    grad_key_raw = grad_key_raw[:, 0].astype(jnp.bfloat16)
    grad_normed_in = jnp.dot(grad_query_raw, w_query.T, preferred_element_type=jnp.float32)
    grad_normed_in = grad_normed_in + jnp.dot(grad_key_raw, w_key.T, preferred_element_type=jnp.float32)
    grad_normed_in = grad_normed_in + jnp.dot(grad_values, w_value.T, preferred_element_type=jnp.float32)
    grad_input_part, grad_gain_in = rms_pull(x_float, in_gain, grad_normed_in)
    grad_inputs = grad_resid + grad_input_part
    pairs = ((normed_in, grad_query_raw), (normed_in, grad_key_raw), (normed_in, grad_values), (attended, grad_attn_proj), (normed_ff, grad_gate), (normed_ff, grad_up), (hidden, grad_ff_proj))
    stacked = tuple(((left.reshape(device_count, TOK_DEV, left.shape[-1]), right.reshape(device_count, TOK_DEV, right.shape[-1])) for left, right in pairs))
    initial = tuple((jnp.zeros((left.shape[-1], right.shape[-1]), jnp.float32) for left, right in pairs))

    def add_device(carry, pieces):
        updated = tuple((total + round_bf16(jnp.dot(piece[0].T, piece[1], preferred_element_type=jnp.float32)) for total, piece in zip(carry, pieces)))
        return (updated, None)
    weight_sums, _ = lax.scan(add_device, initial, stacked)
    grad_w_query, grad_w_key, grad_w_value, grad_w_out, grad_w_gate, grad_w_up, grad_w_down = weight_sums
    return (layer_out, grad_inputs, grad_w_query, grad_w_key, grad_w_value, grad_w_out, grad_w_gate, grad_w_up, grad_w_down, grad_gain_in, grad_gain_attn_post, grad_gain_ff_pre, grad_gain_ff_post, grad_gain_query, grad_gain_key)
```

```python
import functools

import jax
import jax.numpy as jnp
from jax import lax
from jax.experimental import pallas as pl
from jax.experimental.pallas import tpu as pltpu
from jax.sharding import PartitionSpec as P

WINDOW = 512


NORM_EPSILON = 1e-06
ROPE_BASE = 10000.0
MASK_FLOOR = -1e30


def from_behind(array, axis, by):
    count = lax.axis_size(axis)
    pairs = [(i, i + by) for i in range(count) if 0 <= i + by < count]
    return lax.ppermute(array, axis, pairs)


def rms_gain(tensor, gain_vec):
    factor = lax.rsqrt(jnp.mean(tensor * tensor, axis=-1, keepdims=True) + NORM_EPSILON)
    return tensor * factor * (1.0 + gain_vec)


def rope_tables(positions, head_width):
    half_width = head_width // 2
    exponent = jnp.arange(half_width, dtype=jnp.float32) * (2.0 / head_width)
    inverse = jnp.exp(-jnp.log(ROPE_BASE) * exponent)
    angles = positions.astype(jnp.float32)[:, None] * inverse[None, :]
    return (jnp.cos(angles), jnp.sin(angles))


def norm_rope(tensor, gain_vec, cos_table, sin_table):
    normed = rms_gain(tensor, gain_vec)
    half_width = tensor.shape[-1] // 2
    front_part = normed[..., :half_width]
    back_part = normed[..., half_width:]
    cos_rows = cos_table[:, None, :]
    sin_rows = sin_table[:, None, :]
    return jnp.concatenate(
        [
            front_part * cos_rows - back_part * sin_rows,
            back_part * cos_rows + front_part * sin_rows,
        ],
        axis=-1,
    )


def geglu(gate_pre, up_pre):
    return jax.nn.gelu(gate_pre, approximate=True) * up_pre


def window_mask(query_pos, key_pos, query_doc, key_doc):
    distance = query_pos[:, None] - key_pos[None, :]
    return (
        (distance >= 0)
        & (distance < WINDOW)
        & (key_pos[None, :] >= 0)
        & (query_doc[:, None] == key_doc[None, :])
    )


def masked_scores(queries, all_keys, allowed, score_scale):
    scores = (
        jnp.einsum("qhd,kd->hqk", queries, all_keys, preferred_element_type=jnp.float32)
        * score_scale
    )
    return jnp.where(allowed[None], scores, MASK_FLOOR)


def weight_grad(left_rows, right_rows):
    return jnp.einsum("tc,tf->cf", left_rows, right_rows, preferred_element_type=jnp.float32)


MESH = pl.DeviceIdType.MESH
LANES = 128


def coordinates():
    seq = lax.axis_index("seq")
    return lax.rem(seq // 2, 2), lax.rem(seq, 2), seq // 4, lax.axis_index("wshard")


def device(x, core, z, y):
    return ((z * 2 + x) * 2 + core, y)


def greet(partners):
    barrier = pltpu.get_barrier_semaphore()
    for partner in partners:
        pl.semaphore_signal(barrier, inc=1, device_id=partner, device_id_type=MESH)
    pl.semaphore_wait(barrier, len(partners))


def remote(src, dst, send, recv, target):
    return pltpu.make_async_remote_copy(
        src_ref=src, dst_ref=dst, send_sem=send, recv_sem=recv,
        device_id=target, device_id_type=MESH,
    )


def gather_kernel(count, *refs):
    shards, fulls = refs[:count], refs[count : 2 * count]
    own_sem, send_sems, recv_sems = refs[2 * count :]
    x, core, z, y = coordinates()
    sibling = device(x, 1 - core, z, y)
    beside = device(1 - x, core, z, y)
    across = device(x, core, z, 1 - y)
    greet([sibling, beside, across])

    def local(i):
        rows = shards[i].shape[0]
        return pltpu.make_async_copy(
            shards[i], fulls[i].at[pl.ds(y * rows, rows)], own_sem.at[i]
        )

    def first(i):
        rows = shards[i].shape[0]
        part = rows if i == count - 1 else rows // 4
        at = 0 if i == count - 1 else (core * 2 + x) * part
        return remote(
            shards[i].at[pl.ds(at, part)], fulls[i].at[pl.ds(y * rows + at, part)],
            send_sems.at[0, i], recv_sems.at[0, i], across,
        )

    def second(i):
        rows = shards[i].shape[0]
        part = rows // 4
        block = fulls[i].at[pl.ds((1 - y) * rows + (core * 2 + x) * part, part)]
        return remote(block, block, send_sems.at[1, i], recv_sems.at[1, i], beside)

    def third(i):
        rows = shards[i].shape[0]
        part = rows // 2
        block = fulls[i].at[pl.ds((1 - y) * rows + core * part, part)]
        return remote(block, block, send_sems.at[2, i], recv_sems.at[2, i], sibling)

    order = [count - 1] + list(range(count - 1))
    for i in order:
        first(i).start()
    for i in range(count):
        local(i).start()
    first(count - 1).wait_recv()
    big = count - 1
    for step in range(big + 1):
        if step < big:
            first(step).wait_recv()
            second(step).start()
        if step >= 1:
            second(step - 1).wait_recv()
            third(step - 1).start()
    for i in range(big):
        third(i).wait_recv()
    for i in range(count):
        local(i).wait()
        first(i).wait_send()
    for i in range(big):
        second(i).wait_send()
        third(i).wait_send()


def gather_weights(shards):
    count = len(shards)
    return pl.pallas_call(
        functools.partial(gather_kernel, count),
        out_shape=[jax.ShapeDtypeStruct((2 * s.shape[0],) + s.shape[1:], s.dtype) for s in shards],
        in_specs=[pl.BlockSpec(memory_space=pl.ANY)] * count,
        out_specs=[pl.BlockSpec(memory_space=pltpu.VMEM)] * count,
        scratch_shapes=[
            pltpu.SemaphoreType.DMA((count,)),
            pltpu.SemaphoreType.DMA((3, count)),
            pltpu.SemaphoreType.DMA((3, count)),
        ],
        compiler_params=pltpu.CompilerParams(
            collective_id=1, has_side_effects=True, vmem_limit_bytes=48 * 2**20
        ),
        name="gather_weights",
    )(*shards)


def reduce_kernel(
    terms, gains, out, gains_out,
    from_core, from_across, from_beside, from_line, gain_in,
    send_core, recv_core, send_across, recv_across, send_beside, recv_beside,
    send_line, recv_line, send_zline, recv_zline, send_xback, recv_xback,
    send_back, recv_back, send_gain, recv_gain,
):
    chunks = terms.shape[0]
    depth = terms.shape[4]
    x, core, z, y = coordinates()
    sibling = device(x, 1 - core, z, y)
    beside = device(1 - x, core, z, y)
    across = device(x, core, z, 1 - y)
    line = [device(x, core, lax.rem(z + d, depth), y) for d in range(1, depth)]
    greet([sibling, beside, across] + line)

    def to_core(c):
        return remote(terms.at[c, 1 - core], from_core.at[c], send_core.at[c], recv_core.at[c], sibling)

    def to_across(c):
        return remote(
            from_core.at[c, 1 - y], from_across.at[c], send_across.at[c], recv_across.at[c], across
        )

    def to_beside(c):
        return remote(
            from_across.at[c, 1 - x], from_beside.at[c], send_beside.at[c], recv_beside.at[c], beside
        )

    def to_line(c, d):
        return remote(
            from_beside.at[c, lax.rem(z + d, depth)], from_line.at[c, d - 1],
            send_line.at[c, d - 1], recv_line.at[c, d - 1], line[d - 1],
        )

    def along_line(c, d):
        block = out.at[c, core, x, z]
        return remote(block, block, send_zline.at[c, d - 1], recv_zline.at[c, d - 1], line[d - 1])

    def along_line_arrival(c, d):
        block = out.at[c, core, x, lax.rem(z + depth - d, depth)]
        return remote(block, block, send_zline.at[c, d - 1], recv_zline.at[c, d - 1], line[d - 1])

    def back_beside(c, side):
        block = out.at[c, core, side]
        return remote(block, block, send_xback.at[c], recv_xback.at[c], beside)

    def back_core(c, side):
        block = out.at[c, side]
        return remote(block, block, send_back.at[c], recv_back.at[c], sibling)

    def gain_copy(step):
        target = ([sibling, across, beside] + line)[step]
        src = gains if step == 0 else gains_out.at[min(step, 3) - 1]
        return remote(src, gain_in.at[step], send_gain.at[step], recv_gain.at[step], target)

    def add(a, b):
        return (a.astype(jnp.float32) + b.astype(jnp.float32)).astype(jnp.bfloat16)

    @pl.loop(0, chunks)
    def _(c):
        to_core(c).start()

    gain_copy(0).start()

    def stage(at, action):
        @pl.when((at >= 0) & (at < chunks))
        def _():
            action(at)

    def after_core(c):
        to_core(c).wait_recv()
        from_core[c, 1 - y] = add(from_core[c, 1 - y], terms[c, core, 1 - y])
        to_across(c).start()
        from_core[c, y] = add(from_core[c, y], terms[c, core, y])

    def after_across(c):
        to_across(c).wait_recv()
        from_across[c, 1 - x] = add(from_across[c, 1 - x], from_core[c, y, 1 - x])
        to_beside(c).start()
        from_across[c, x] = add(from_across[c, x], from_core[c, y, x])

    def after_beside(c):
        to_beside(c).wait_recv()
        from_beside[c] = add(from_beside[c], from_across[c, x])
        for d in range(1, depth):
            to_line(c, d).start()

    def after_line(c):
        total = from_beside[c, z].astype(jnp.float32)
        for d in range(1, depth):
            to_line(c, d).wait_recv()
            total = total + from_line[c, d - 1].astype(jnp.float32)
        out[c, core, x, z] = total.astype(jnp.bfloat16)
        for d in range(1, depth):
            along_line(c, d).start()

    def after_zline(c):
        for d in range(1, depth):
            along_line_arrival(c, d).wait_recv()
        back_beside(c, x).start()

    def after_xback(c):
        back_beside(c, 1 - x).wait_recv()
        back_core(c, core).start()

    actions = [after_core, after_across, after_beside, after_line, after_zline, after_xback]

    @pl.loop(0, chunks + len(actions) - 1)
    def _(t):
        for lag, action in enumerate(actions):
            stage(t - lag, action)
        for step in range(3):
            @pl.when(t == step + 1)
            def _():
                gain_copy(step).wait_recv()
                before = gains[...] if step == 0 else gains_out[step - 1]
                gains_out[step] = before + gain_in[step]
                if step < 2:
                    gain_copy(step + 1).start()
                else:
                    for d in range(1, depth):
                        gain_copy(2 + d).start()

    total = gains_out[2]
    for d in range(1, depth):
        gain_copy(2 + d).wait_recv()
        total = total + gain_in[2 + d]
    gains_out[3] = total
    for step in range(2 + depth):
        gain_copy(step).wait_send()

    @pl.loop(0, chunks)
    def _(c):
        back_core(c, 1 - core).wait_recv()
        to_core(c).wait_send()
        to_across(c).wait_send()
        to_beside(c).wait_send()
        for d in range(1, depth):
            to_line(c, d).wait_send()
            along_line(c, d).wait_send()
        back_beside(c, x).wait_send()
        back_core(c, core).wait_send()


def reduce_terms(terms, gains):
    chunks, _, _, _, depth, rows, lanes = terms.shape
    piece = (rows, lanes)
    dma = pltpu.SemaphoreType.DMA
    vmem = pl.BlockSpec(memory_space=pltpu.VMEM)
    pair = [dma((chunks,)), dma((chunks,))]
    lines = [dma((chunks, depth - 1)), dma((chunks, depth - 1))]
    steps = 2 + depth
    return pl.pallas_call(
        reduce_kernel,
        out_shape=[
            jax.ShapeDtypeStruct((chunks, 2, 2, depth) + piece, jnp.bfloat16),
            jax.ShapeDtypeStruct((4,) + gains.shape, jnp.float32),
        ],
        in_specs=[vmem, vmem],
        out_specs=[vmem, vmem],
        scratch_shapes=[
            pltpu.VMEM((chunks, 2, 2, depth) + piece, jnp.bfloat16),
            pltpu.VMEM((chunks, 2, depth) + piece, jnp.bfloat16),
            pltpu.VMEM((chunks, depth) + piece, jnp.bfloat16),
            pltpu.VMEM((chunks, depth - 1) + piece, jnp.bfloat16),
            pltpu.VMEM((steps,) + gains.shape, jnp.float32),
        ]
        + pair + pair + pair + lines + lines + pair + pair
        + [dma((steps,)), dma((steps,))],
        compiler_params=pltpu.CompilerParams(
            collective_id=2, has_side_effects=True, vmem_limit_bytes=48 * 2**20
        ),
        name="reduce_terms",
    )(terms, gains)


def split_columns(term, depth):
    rows, columns = term.shape
    term = term.reshape(2, 2, 2, rows // 8, columns // (depth * LANES), depth, LANES)
    return term.transpose(4, 1, 0, 2, 5, 3, 6)


def join_columns(pieces):
    chunks, _, _, depth, rows, lanes = pieces.shape
    return pieces.transpose(1, 2, 4, 0, 3, 5).reshape(4 * rows, chunks * depth * lanes)


def split_rows(term, depth, piece_rows):
    rows, columns = term.shape
    tiles = columns // LANES
    high = piece_rows // tiles
    chunks = rows // (8 * depth * high)
    term = term.reshape(2, chunks, 2, 2, depth, high, tiles, LANES)
    term = term.transpose(1, 2, 0, 3, 4, 6, 5, 7)
    return term.reshape(chunks, 2, 2, 2, depth, tiles * high, LANES)


def join_rows(pieces, columns):
    chunks, _, _, depth, piece_rows, lanes = pieces.shape
    tiles = columns // lanes
    high = piece_rows // tiles
    pieces = pieces.reshape(chunks, 2, 2, depth, tiles, high, lanes).transpose(0, 1, 2, 3, 5, 4, 6)
    return pieces.reshape(chunks * 4 * depth * high, columns)


def per_device(
    inputs,
    doc_ids,
    w_query,
    w_key,
    w_value,
    w_out,
    w_gate,
    w_up,
    w_down,
    gain_in,
    gain_attn_post,
    gain_ff_pre,
    gain_ff_post,
    gain_query,
    gain_key,
    cotangent,
):
    small = (gain_in, gain_attn_post, gain_ff_pre, gain_ff_post, gain_query, gain_key)
    small_shard = jnp.concatenate(small).astype(jnp.float32).reshape(1, -1, LANES)
    gathered = gather_weights(
        (w_query, w_key, w_value, w_out, w_gate, w_up, w_down, small_shard)
    )
    full_query, full_key, full_value, full_out, full_gate, full_up, full_down = gathered[:7]
    small_full = gathered[7].reshape(2, -1)
    starts = [0]
    for vec in small:
        starts.append(starts[-1] + vec.shape[0])
    in_gain, attn_post_gain, ff_pre_gain, ff_post_gain, query_gain, key_gain = [
        small_full[:, low:high].reshape(-1) for low, high in zip(starts[:-1], starts[1:])
    ]
    row_count = inputs.shape[0]
    head_dim = full_key.shape[1]
    head_count = full_query.shape[1] // head_dim
    score_scale = head_dim ** (-0.5)
    start_row = lax.axis_index(("seq", "wshard")) * row_count
    query_pos = start_row + jnp.arange(row_count, dtype=jnp.int32)
    cos_table, sin_table = rope_tables(query_pos, head_dim)
    x_float = inputs.astype(jnp.float32)
    normed_in = rms_gain(x_float, in_gain).astype(jnp.bfloat16)
    query_raw = jnp.dot(normed_in, full_query, preferred_element_type=jnp.float32).reshape(
        row_count, head_count, head_dim
    )
    key_raw = jnp.dot(normed_in, full_key, preferred_element_type=jnp.float32)[:, None, :]
    values = jnp.dot(normed_in, full_value, preferred_element_type=jnp.float32).astype(jnp.bfloat16)
    queries = norm_rope(query_raw, query_gain, cos_table, sin_table).astype(jnp.bfloat16)
    key_rot = norm_rope(key_raw, key_gain, cos_table, sin_table)[:, 0].astype(jnp.bfloat16)
    sent_rows = min(WINDOW, row_count)
    hop_count = WINDOW // sent_rows
    outgoing = (key_rot, values, doc_ids)
    halo_keys = []
    halo_values = []
    halo_docs = []
    for distance in range(hop_count, 0, -1):
        arrived = from_behind((outgoing[0], outgoing[1], outgoing[2]), ("seq", "wshard"), distance)
        halo_keys.append(arrived[0])
        halo_values.append(arrived[1])
        halo_docs.append(arrived[2])
    all_keys = jnp.concatenate(halo_keys + [key_rot], 0)
    all_values = jnp.concatenate(halo_values + [values], 0)
    all_docs = jnp.concatenate(halo_docs + [doc_ids], 0)
    key_pos = start_row - WINDOW + jnp.arange(WINDOW + row_count, dtype=jnp.int32)
    allowed = window_mask(query_pos, key_pos, doc_ids, all_docs)
    scores = masked_scores(queries, all_keys, allowed, score_scale)
    row_peak = jnp.max(scores, axis=-1, keepdims=True)
    row_total = jnp.sum(
        jnp.where(allowed[None], jnp.exp(scores - row_peak), 0.0), axis=-1, keepdims=True
    )
    log_total = row_peak + jnp.log(row_total)
    soft = jnp.where(allowed[None], jnp.exp(scores - log_total), 0.0).astype(jnp.bfloat16)
    attended = jnp.einsum("hqk,kd->qhd", soft, all_values, preferred_element_type=jnp.float32)
    attended = attended.reshape(row_count, head_count * head_dim).astype(jnp.bfloat16)
    attn_proj = jnp.dot(attended, full_out, preferred_element_type=jnp.float32)
    resid = x_float + rms_gain(attn_proj, attn_post_gain)
    normed_ff = rms_gain(resid, ff_pre_gain).astype(jnp.bfloat16)
    gate_pre = jnp.dot(normed_ff, full_gate, preferred_element_type=jnp.float32)
    up_pre = jnp.dot(normed_ff, full_up, preferred_element_type=jnp.float32)
    hidden = geglu(gate_pre, up_pre).astype(jnp.bfloat16)
    ff_proj = jnp.dot(hidden, full_down, preferred_element_type=jnp.float32)
    layer_out = (resid + rms_gain(ff_proj, ff_post_gain)).astype(jnp.bfloat16)
    grad_top = cotangent.astype(jnp.float32)
    _, pullback = jax.vjp(rms_gain, ff_proj, ff_post_gain)
    grad_ff_proj, grad_gain_ff_post = pullback(grad_top)
    grad_ff_proj = grad_ff_proj.astype(jnp.bfloat16)
    grad_w_down = weight_grad(hidden, grad_ff_proj)
    grad_hidden = lax.dot_general(
        grad_ff_proj, full_down, (((1,), (1,)), ((), ())), preferred_element_type=jnp.float32
    )
    _, pullback = jax.vjp(geglu, gate_pre, up_pre)
    grad_gate, grad_up = pullback(grad_hidden)
    grad_gate = grad_gate.astype(jnp.bfloat16)
    grad_up = grad_up.astype(jnp.bfloat16)
    grad_w_gate = weight_grad(normed_ff, grad_gate)
    grad_w_up = weight_grad(normed_ff, grad_up)
    grad_normed_ff = lax.dot_general(
        grad_gate, full_gate, (((1,), (1,)), ((), ())), preferred_element_type=jnp.float32
    )
    grad_normed_ff = grad_normed_ff + lax.dot_general(
        grad_up, full_up, (((1,), (1,)), ((), ())), preferred_element_type=jnp.float32
    )
    _, pullback = jax.vjp(rms_gain, resid, ff_pre_gain)
    grad_resid_part, grad_gain_ff_pre = pullback(grad_normed_ff)
    grad_resid = grad_top + grad_resid_part
    ff_gradients = (grad_w_gate, grad_w_up, grad_w_down, grad_gain_ff_pre, grad_gain_ff_post)
    _, pullback = jax.vjp(rms_gain, attn_proj, attn_post_gain)
    grad_attn_proj, grad_gain_attn_post = pullback(grad_resid)
    grad_attn_proj = grad_attn_proj.astype(jnp.bfloat16)
    grad_w_out = weight_grad(attended, grad_attn_proj)
    grad_attended = lax.dot_general(
        grad_attn_proj, full_out, (((1,), (1,)), ((), ())), preferred_element_type=jnp.float32
    ).astype(jnp.bfloat16)
    grad_heads = grad_attended.reshape(row_count, head_count, head_dim)
    again_scores = masked_scores(queries, all_keys, allowed, score_scale)
    probs = jnp.where(allowed[None], jnp.exp(again_scores - log_total), 0.0)
    grad_soft = jnp.einsum(
        "qhd,kd->hqk", grad_heads, all_values, preferred_element_type=jnp.float32
    )
    row_inner = jnp.sum(probs * grad_soft, axis=-1, keepdims=True)
    grad_score = (probs * (grad_soft - row_inner) * score_scale).astype(jnp.bfloat16)
    grad_queries = jnp.einsum(
        "hqk,kd->qhd", grad_score, all_keys, preferred_element_type=jnp.float32
    )
    grad_keys_all = jnp.einsum(
        "hqk,qhd->kd", grad_score, queries, preferred_element_type=jnp.float32
    )
    grad_values_all = jnp.einsum(
        "hqk,qhd->kd", probs.astype(jnp.bfloat16), grad_heads, preferred_element_type=jnp.float32
    )
    back_keys = jnp.zeros((sent_rows, head_dim), jnp.float32)
    back_values = jnp.zeros((sent_rows, head_dim), jnp.float32)
    for piece_index in range(hop_count):
        distance = hop_count - piece_index
        piece_start = piece_index * sent_rows
        arrived = (
            from_behind(
                grad_keys_all[piece_start : piece_start + sent_rows].astype(jnp.bfloat16),
                ("seq", "wshard"),
                -distance,
            ).astype(jnp.float32),
            from_behind(
                grad_values_all[piece_start : piece_start + sent_rows].astype(jnp.bfloat16),
                ("seq", "wshard"),
                -distance,
            ).astype(jnp.float32),
        )
        back_keys = back_keys + arrived[0]
        back_values = back_values + arrived[1]
    own_keys = grad_keys_all[WINDOW:]
    own_values = grad_values_all[WINDOW:]
    split_row = row_count - sent_rows
    grad_keys = jnp.concatenate([own_keys[:split_row], own_keys + back_keys], 0)
    grad_values = jnp.concatenate([own_values[:split_row], own_values + back_values], 0).astype(
        jnp.bfloat16
    )

    def query_path(tensor, gain_vec):
        return norm_rope(tensor, gain_vec, cos_table, sin_table)

    _, pullback = jax.vjp(query_path, query_raw, query_gain)
    grad_query_raw, grad_gain_query = pullback(grad_queries)
    _, pullback = jax.vjp(query_path, key_raw, key_gain)
    grad_key_raw, grad_gain_key = pullback(grad_keys[:, None, :])
    grad_query_raw = grad_query_raw.reshape(row_count, head_count * head_dim).astype(jnp.bfloat16)
    grad_key_raw = grad_key_raw[:, 0].astype(jnp.bfloat16)
    grad_w_query = weight_grad(normed_in, grad_query_raw)
    grad_w_key = weight_grad(normed_in, grad_key_raw)
    grad_w_value = weight_grad(normed_in, grad_values)
    grad_normed_in = lax.dot_general(
        grad_query_raw, full_query, (((1,), (1,)), ((), ())), preferred_element_type=jnp.float32
    )
    grad_normed_in = grad_normed_in + lax.dot_general(
        grad_key_raw, full_key, (((1,), (1,)), ((), ())), preferred_element_type=jnp.float32
    )
    grad_normed_in = grad_normed_in + lax.dot_general(
        grad_values, full_value, (((1,), (1,)), ((), ())), preferred_element_type=jnp.float32
    )
    _, pullback = jax.vjp(rms_gain, x_float, in_gain)
    grad_input_part, grad_gain_in = pullback(grad_normed_in)
    grad_inputs = grad_resid + grad_input_part
    attn_gradients = (
        grad_w_query,
        grad_w_key,
        grad_w_value,
        grad_w_out,
        grad_gain_in,
        grad_gain_attn_post,
        grad_gain_query,
        grad_gain_key,
    )
    depth = lax.axis_size("seq") // 4
    bf16 = [g.astype(jnp.bfloat16) for g in attn_gradients[:4] + ff_gradients[:3]]
    by_columns = [
        bf16[4], bf16[5], bf16[0], jnp.concatenate([bf16[1], bf16[2]], axis=1)
    ]
    pieces = [split_columns(g, depth) for g in by_columns]
    piece_rows = pieces[0].shape[5]
    by_rows = [bf16[6], bf16[3]]
    pieces = pieces[:2] + [split_rows(by_rows[0], depth, piece_rows)] + pieces[2:]
    pieces = pieces + [split_rows(by_rows[1], depth, piece_rows)]
    gain_terms = attn_gradients[4:6] + ff_gradients[3:5] + attn_gradients[6:8]
    gain_rows = jnp.concatenate(gain_terms).astype(jnp.bfloat16).astype(jnp.float32)
    summed, gain_sums = reduce_terms(
        jnp.concatenate(pieces, axis=0), gain_rows.reshape(-1, LANES)
    )
    bounds = [0]
    for piece in pieces:
        bounds.append(bounds[-1] + piece.shape[0])
    cuts = [summed[low:high].astype(jnp.float32) for low, high in zip(bounds[:-1], bounds[1:])]
    sum_gate, sum_up, sum_query, sum_key_value = [
        join_columns(cuts[i]) for i in (0, 1, 3, 4)
    ]
    sum_down = join_rows(cuts[2], by_rows[0].shape[1])
    sum_out = join_rows(cuts[5], by_rows[1].shape[1])
    me = lax.axis_index("wshard")
    gain_sums = gain_sums[3].reshape(-1)
    gain_outs = []
    start = 0
    for term in gain_terms:
        half = term.shape[0] // 2
        gain_outs.append(lax.dynamic_slice_in_dim(gain_sums, start + me * half, half))
        start += term.shape[0]
    return (
        layer_out, grad_inputs, sum_query, sum_key_value[:, :head_dim], sum_key_value[:, head_dim:],
        sum_out, sum_gate, sum_up, sum_down,
    ) + tuple(gain_outs)


def per_device_general(
    inputs,
    doc_ids,
    w_query,
    w_key,
    w_value,
    w_out,
    w_gate,
    w_up,
    w_down,
    gain_in,
    gain_attn_post,
    gain_ff_pre,
    gain_ff_post,
    gain_query,
    gain_key,
    cotangent,
):
    gathered = (
        lax.all_gather(w_query, "wshard", axis=0, tiled=True),
        lax.all_gather(w_key, "wshard", axis=0, tiled=True),
        lax.all_gather(w_value, "wshard", axis=0, tiled=True),
        lax.all_gather(w_out, "wshard", axis=0, tiled=True),
        lax.all_gather(w_gate, "wshard", axis=0, tiled=True),
        lax.all_gather(w_up, "wshard", axis=0, tiled=True),
        lax.all_gather(w_down, "wshard", axis=0, tiled=True),
        lax.all_gather(gain_in, "wshard", axis=0, tiled=True),
        lax.all_gather(gain_attn_post, "wshard", axis=0, tiled=True),
        lax.all_gather(gain_ff_pre, "wshard", axis=0, tiled=True),
        lax.all_gather(gain_ff_post, "wshard", axis=0, tiled=True),
        lax.all_gather(gain_query, "wshard", axis=0, tiled=True),
        lax.all_gather(gain_key, "wshard", axis=0, tiled=True),
    )
    full_query, full_key, full_value, full_out, full_gate, full_up, full_down = gathered[:7]
    in_gain, attn_post_gain, ff_pre_gain, ff_post_gain, query_gain, key_gain = [
        g.astype(jnp.float32) for g in gathered[7:]
    ]
    row_count = inputs.shape[0]
    head_dim = full_key.shape[1]
    head_count = full_query.shape[1] // head_dim
    score_scale = head_dim ** (-0.5)
    start_row = lax.axis_index(("seq", "wshard")) * row_count
    query_pos = start_row + jnp.arange(row_count, dtype=jnp.int32)
    cos_table, sin_table = rope_tables(query_pos, head_dim)
    x_float = inputs.astype(jnp.float32)
    normed_in = rms_gain(x_float, in_gain).astype(jnp.bfloat16)
    query_raw = jnp.dot(normed_in, full_query, preferred_element_type=jnp.float32).reshape(
        row_count, head_count, head_dim
    )
    key_raw = jnp.dot(normed_in, full_key, preferred_element_type=jnp.float32)[:, None, :]
    values = jnp.dot(normed_in, full_value, preferred_element_type=jnp.float32).astype(jnp.bfloat16)
    queries = norm_rope(query_raw, query_gain, cos_table, sin_table).astype(jnp.bfloat16)
    key_rot = norm_rope(key_raw, key_gain, cos_table, sin_table)[:, 0].astype(jnp.bfloat16)
    sent_rows = min(WINDOW, row_count)
    hop_count = WINDOW // sent_rows
    outgoing = (key_rot, values, doc_ids)
    halo_keys = []
    halo_values = []
    halo_docs = []
    for distance in range(hop_count, 0, -1):
        arrived = from_behind((outgoing[0], outgoing[1], outgoing[2]), ("seq", "wshard"), distance)
        halo_keys.append(arrived[0])
        halo_values.append(arrived[1])
        halo_docs.append(arrived[2])
    all_keys = jnp.concatenate(halo_keys + [key_rot], 0)
    all_values = jnp.concatenate(halo_values + [values], 0)
    all_docs = jnp.concatenate(halo_docs + [doc_ids], 0)
    key_pos = start_row - WINDOW + jnp.arange(WINDOW + row_count, dtype=jnp.int32)
    allowed = window_mask(query_pos, key_pos, doc_ids, all_docs)
    scores = masked_scores(queries, all_keys, allowed, score_scale)
    row_peak = jnp.max(scores, axis=-1, keepdims=True)
    row_total = jnp.sum(
        jnp.where(allowed[None], jnp.exp(scores - row_peak), 0.0), axis=-1, keepdims=True
    )
    log_total = row_peak + jnp.log(row_total)
    soft = jnp.where(allowed[None], jnp.exp(scores - log_total), 0.0).astype(jnp.bfloat16)
    attended = jnp.einsum("hqk,kd->qhd", soft, all_values, preferred_element_type=jnp.float32)
    attended = attended.reshape(row_count, head_count * head_dim).astype(jnp.bfloat16)
    attn_proj = jnp.dot(attended, full_out, preferred_element_type=jnp.float32)
    resid = x_float + rms_gain(attn_proj, attn_post_gain)
    normed_ff = rms_gain(resid, ff_pre_gain).astype(jnp.bfloat16)
    gate_pre = jnp.dot(normed_ff, full_gate, preferred_element_type=jnp.float32)
    up_pre = jnp.dot(normed_ff, full_up, preferred_element_type=jnp.float32)
    hidden = geglu(gate_pre, up_pre).astype(jnp.bfloat16)
    ff_proj = jnp.dot(hidden, full_down, preferred_element_type=jnp.float32)
    layer_out = (resid + rms_gain(ff_proj, ff_post_gain)).astype(jnp.bfloat16)
    grad_top = cotangent.astype(jnp.float32)
    _, pullback = jax.vjp(rms_gain, ff_proj, ff_post_gain)
    grad_ff_proj, grad_gain_ff_post = pullback(grad_top)
    grad_ff_proj = grad_ff_proj.astype(jnp.bfloat16)
    grad_w_down = weight_grad(hidden, grad_ff_proj)
    grad_hidden = lax.dot_general(
        grad_ff_proj, full_down, (((1,), (1,)), ((), ())), preferred_element_type=jnp.float32
    )
    _, pullback = jax.vjp(geglu, gate_pre, up_pre)
    grad_gate, grad_up = pullback(grad_hidden)
    grad_gate = grad_gate.astype(jnp.bfloat16)
    grad_up = grad_up.astype(jnp.bfloat16)
    grad_w_gate = weight_grad(normed_ff, grad_gate)
    grad_w_up = weight_grad(normed_ff, grad_up)
    grad_normed_ff = lax.dot_general(
        grad_gate, full_gate, (((1,), (1,)), ((), ())), preferred_element_type=jnp.float32
    )
    grad_normed_ff = grad_normed_ff + lax.dot_general(
        grad_up, full_up, (((1,), (1,)), ((), ())), preferred_element_type=jnp.float32
    )
    _, pullback = jax.vjp(rms_gain, resid, ff_pre_gain)
    grad_resid_part, grad_gain_ff_pre = pullback(grad_normed_ff)
    grad_resid = grad_top + grad_resid_part
    ff_gradients = (grad_w_gate, grad_w_up, grad_w_down, grad_gain_ff_pre, grad_gain_ff_post)
    ff_parts = (
        lax.psum_scatter(
            ff_gradients[0].astype(jnp.bfloat16), "wshard", scatter_dimension=0, tiled=True
        ).astype(jnp.float32),
        lax.psum_scatter(
            ff_gradients[1].astype(jnp.bfloat16), "wshard", scatter_dimension=0, tiled=True
        ).astype(jnp.float32),
        lax.psum_scatter(
            ff_gradients[2].astype(jnp.bfloat16), "wshard", scatter_dimension=0, tiled=True
        ).astype(jnp.float32),
        lax.psum_scatter(
            ff_gradients[3].astype(jnp.bfloat16), "wshard", scatter_dimension=0, tiled=True
        ).astype(jnp.float32),
        lax.psum_scatter(
            ff_gradients[4].astype(jnp.bfloat16), "wshard", scatter_dimension=0, tiled=True
        ).astype(jnp.float32),
    )
    ff_reduced = (
        lax.psum(ff_parts[0].astype(jnp.bfloat16), "seq").astype(jnp.float32),
        lax.psum(ff_parts[1].astype(jnp.bfloat16), "seq").astype(jnp.float32),
        lax.psum(ff_parts[2].astype(jnp.bfloat16), "seq").astype(jnp.float32),
        lax.psum(ff_parts[3].astype(jnp.bfloat16), "seq").astype(jnp.float32),
        lax.psum(ff_parts[4].astype(jnp.bfloat16), "seq").astype(jnp.float32),
    )
    _, pullback = jax.vjp(rms_gain, attn_proj, attn_post_gain)
    grad_attn_proj, grad_gain_attn_post = pullback(grad_resid)
    grad_attn_proj = grad_attn_proj.astype(jnp.bfloat16)
    grad_w_out = weight_grad(attended, grad_attn_proj)
    grad_attended = lax.dot_general(
        grad_attn_proj, full_out, (((1,), (1,)), ((), ())), preferred_element_type=jnp.float32
    ).astype(jnp.bfloat16)
    grad_heads = grad_attended.reshape(row_count, head_count, head_dim)
    again_scores = masked_scores(queries, all_keys, allowed, score_scale)
    probs = jnp.where(allowed[None], jnp.exp(again_scores - log_total), 0.0)
    grad_soft = jnp.einsum(
        "qhd,kd->hqk", grad_heads, all_values, preferred_element_type=jnp.float32
    )
    row_inner = jnp.sum(probs * grad_soft, axis=-1, keepdims=True)
    grad_score = (probs * (grad_soft - row_inner) * score_scale).astype(jnp.bfloat16)
    grad_queries = jnp.einsum(
        "hqk,kd->qhd", grad_score, all_keys, preferred_element_type=jnp.float32
    )
    grad_keys_all = jnp.einsum(
        "hqk,qhd->kd", grad_score, queries, preferred_element_type=jnp.float32
    )
    grad_values_all = jnp.einsum(
        "hqk,qhd->kd", probs.astype(jnp.bfloat16), grad_heads, preferred_element_type=jnp.float32
    )
    back_keys = jnp.zeros((sent_rows, head_dim), jnp.float32)
    back_values = jnp.zeros((sent_rows, head_dim), jnp.float32)
    for piece_index in range(hop_count):
        distance = hop_count - piece_index
        piece_start = piece_index * sent_rows
        arrived = (
            from_behind(
                grad_keys_all[piece_start : piece_start + sent_rows].astype(jnp.bfloat16),
                ("seq", "wshard"),
                -distance,
            ).astype(jnp.float32),
            from_behind(
                grad_values_all[piece_start : piece_start + sent_rows].astype(jnp.bfloat16),
                ("seq", "wshard"),
                -distance,
            ).astype(jnp.float32),
        )
        back_keys = back_keys + arrived[0]
        back_values = back_values + arrived[1]
    own_keys = grad_keys_all[WINDOW:]
    own_values = grad_values_all[WINDOW:]
    split_row = row_count - sent_rows
    grad_keys = jnp.concatenate([own_keys[:split_row], own_keys + back_keys], 0)
    grad_values = jnp.concatenate([own_values[:split_row], own_values + back_values], 0).astype(
        jnp.bfloat16
    )

    def query_path(tensor, gain_vec):
        return norm_rope(tensor, gain_vec, cos_table, sin_table)

    _, pullback = jax.vjp(query_path, query_raw, query_gain)
    grad_query_raw, grad_gain_query = pullback(grad_queries)
    _, pullback = jax.vjp(query_path, key_raw, key_gain)
    grad_key_raw, grad_gain_key = pullback(grad_keys[:, None, :])
    grad_query_raw = grad_query_raw.reshape(row_count, head_count * head_dim).astype(jnp.bfloat16)
    grad_key_raw = grad_key_raw[:, 0].astype(jnp.bfloat16)
    grad_w_query = weight_grad(normed_in, grad_query_raw)
    grad_w_key = weight_grad(normed_in, grad_key_raw)
    grad_w_value = weight_grad(normed_in, grad_values)
    grad_normed_in = lax.dot_general(
        grad_query_raw, full_query, (((1,), (1,)), ((), ())), preferred_element_type=jnp.float32
    )
    grad_normed_in = grad_normed_in + lax.dot_general(
        grad_key_raw, full_key, (((1,), (1,)), ((), ())), preferred_element_type=jnp.float32
    )
    grad_normed_in = grad_normed_in + lax.dot_general(
        grad_values, full_value, (((1,), (1,)), ((), ())), preferred_element_type=jnp.float32
    )
    _, pullback = jax.vjp(rms_gain, x_float, in_gain)
    grad_input_part, grad_gain_in = pullback(grad_normed_in)
    grad_inputs = grad_resid + grad_input_part
    attn_gradients = (
        grad_w_query,
        grad_w_key,
        grad_w_value,
        grad_w_out,
        grad_gain_in,
        grad_gain_attn_post,
        grad_gain_query,
        grad_gain_key,
    )
    attn_parts = (
        lax.psum_scatter(
            attn_gradients[0].astype(jnp.bfloat16), "wshard", scatter_dimension=0, tiled=True
        ).astype(jnp.float32),
        lax.psum_scatter(
            attn_gradients[1].astype(jnp.bfloat16), "wshard", scatter_dimension=0, tiled=True
        ).astype(jnp.float32),
        lax.psum_scatter(
            attn_gradients[2].astype(jnp.bfloat16), "wshard", scatter_dimension=0, tiled=True
        ).astype(jnp.float32),
        lax.psum_scatter(
            attn_gradients[3].astype(jnp.bfloat16), "wshard", scatter_dimension=0, tiled=True
        ).astype(jnp.float32),
        lax.psum_scatter(
            attn_gradients[4].astype(jnp.bfloat16), "wshard", scatter_dimension=0, tiled=True
        ).astype(jnp.float32),
        lax.psum_scatter(
            attn_gradients[5].astype(jnp.bfloat16), "wshard", scatter_dimension=0, tiled=True
        ).astype(jnp.float32),
        lax.psum_scatter(
            attn_gradients[6].astype(jnp.bfloat16), "wshard", scatter_dimension=0, tiled=True
        ).astype(jnp.float32),
        lax.psum_scatter(
            attn_gradients[7].astype(jnp.bfloat16), "wshard", scatter_dimension=0, tiled=True
        ).astype(jnp.float32),
    )
    attn_reduced = (
        lax.psum(attn_parts[0].astype(jnp.bfloat16), "seq").astype(jnp.float32),
        lax.psum(attn_parts[1].astype(jnp.bfloat16), "seq").astype(jnp.float32),
        lax.psum(attn_parts[2].astype(jnp.bfloat16), "seq").astype(jnp.float32),
        lax.psum(attn_parts[3].astype(jnp.bfloat16), "seq").astype(jnp.float32),
        lax.psum(attn_parts[4].astype(jnp.bfloat16), "seq").astype(jnp.float32),
        lax.psum(attn_parts[5].astype(jnp.bfloat16), "seq").astype(jnp.float32),
        lax.psum(attn_parts[6].astype(jnp.bfloat16), "seq").astype(jnp.float32),
        lax.psum(attn_parts[7].astype(jnp.bfloat16), "seq").astype(jnp.float32),
    )
    reduced = (
        attn_reduced[0],
        attn_reduced[1],
        attn_reduced[2],
        attn_reduced[3],
        ff_reduced[0],
        ff_reduced[1],
        ff_reduced[2],
        attn_reduced[4],
        attn_reduced[5],
        ff_reduced[3],
        ff_reduced[4],
        attn_reduced[6],
        attn_reduced[7],
    )
    return (layer_out, grad_inputs) + tuple(reduced)


def solution(mesh):
    routed = mesh.shape["wshard"] == 2 and mesh.shape["seq"] == 16
    return jax.shard_map(
        per_device if routed else per_device_general,
        mesh=mesh,
        in_specs=(
            P(("seq", "wshard"), None),
            P(("seq", "wshard")),
            P("wshard", None),
            P("wshard", None),
            P("wshard", None),
            P("wshard", None),
            P("wshard", None),
            P("wshard", None),
            P("wshard", None),
            P("wshard"),
            P("wshard"),
            P("wshard"),
            P("wshard"),
            P("wshard"),
            P("wshard"),
            P(("seq", "wshard"), None),
        ),
        out_specs=(
            P(("seq", "wshard"), None),
            P(("seq", "wshard"), None),
            P("wshard", None),
            P("wshard", None),
            P("wshard", None),
            P("wshard", None),
            P("wshard", None),
            P("wshard", None),
            P("wshard", None),
            P("wshard"),
            P("wshard"),
            P("wshard"),
            P("wshard"),
            P("wshard"),
            P("wshard"),
        ),
        check_vma=False,
    )
```

```python
import functools

import jax
import jax.numpy as jnp
from jax import lax
from jax.experimental import pallas as pl
from jax.experimental.pallas import tpu as pltpu
from jax.sharding import PartitionSpec as P

WINDOW = 512


NORM_EPSILON = 1e-06
ROPE_BASE = 10000.0
MASK_FLOOR = -1e30


def from_behind(array, axis, by):
    count = lax.axis_size(axis)
    pairs = [(i, i + by) for i in range(count) if 0 <= i + by < count]
    return lax.ppermute(array, axis, pairs)


def rms_gain(tensor, gain_vec):
    factor = lax.rsqrt(jnp.mean(tensor * tensor, axis=-1, keepdims=True) + NORM_EPSILON)
    return tensor * factor * (1.0 + gain_vec)


def rope_tables(positions, head_width):
    half_width = head_width // 2
    exponent = jnp.arange(half_width, dtype=jnp.float32) * (2.0 / head_width)
    inverse = jnp.exp(-jnp.log(ROPE_BASE) * exponent)
    angles = positions.astype(jnp.float32)[:, None] * inverse[None, :]
    return (jnp.cos(angles), jnp.sin(angles))


def norm_rope(tensor, gain_vec, cos_table, sin_table):
    normed = rms_gain(tensor, gain_vec)
    half_width = tensor.shape[-1] // 2
    front_part = normed[..., :half_width]
    back_part = normed[..., half_width:]
    cos_rows = cos_table[:, None, :]
    sin_rows = sin_table[:, None, :]
    return jnp.concatenate(
        [
            front_part * cos_rows - back_part * sin_rows,
            back_part * cos_rows + front_part * sin_rows,
        ],
        axis=-1,
    )


def geglu(gate_pre, up_pre):
    return jax.nn.gelu(gate_pre, approximate=True) * up_pre


def window_mask(query_pos, key_pos, query_doc, key_doc):
    distance = query_pos[:, None] - key_pos[None, :]
    return (
        (distance >= 0)
        & (distance < WINDOW)
        & (key_pos[None, :] >= 0)
        & (query_doc[:, None] == key_doc[None, :])
    )


def masked_scores(queries, all_keys, allowed, score_scale):
    scores = (
        jnp.einsum("qhd,kd->hqk", queries, all_keys, preferred_element_type=jnp.float32)
        * score_scale
    )
    return jnp.where(allowed[None], scores, MASK_FLOOR)


def weight_grad(left_rows, right_rows):
    return jnp.einsum("tc,tf->cf", left_rows, right_rows, preferred_element_type=jnp.float32)


MESH = pl.DeviceIdType.MESH
LANES = 128


def coordinates():
    seq = lax.axis_index("seq")
    return lax.rem(seq // 2, 2), lax.rem(seq, 2), seq // 4, lax.axis_index("wshard")


def device(x, core, z, y):
    return ((z * 2 + x) * 2 + core, y)


def greet(partners):
    barrier = pltpu.get_barrier_semaphore()
    for partner in partners:
        pl.semaphore_signal(barrier, inc=1, device_id=partner, device_id_type=MESH)
    pl.semaphore_wait(barrier, len(partners))


def remote(src, dst, send, recv, target):
    return pltpu.make_async_remote_copy(
        src_ref=src, dst_ref=dst, send_sem=send, recv_sem=recv,
        device_id=target, device_id_type=MESH,
    )


def gather_kernel(count, *refs):
    shards, fulls = refs[:count], refs[count : 2 * count]
    own_sem, send_sems, recv_sems = refs[2 * count :]
    x, core, z, y = coordinates()
    sibling = device(x, 1 - core, z, y)
    beside = device(1 - x, core, z, y)
    across = device(x, core, z, 1 - y)
    greet([sibling, beside, across])

    def local(i):
        rows = shards[i].shape[0]
        return pltpu.make_async_copy(
            shards[i], fulls[i].at[pl.ds(y * rows, rows)], own_sem.at[i]
        )

    def first(i):
        rows = shards[i].shape[0]
        part = rows if i == count - 1 else rows // 4
        at = 0 if i == count - 1 else (core * 2 + x) * part
        return remote(
            shards[i].at[pl.ds(at, part)], fulls[i].at[pl.ds(y * rows + at, part)],
            send_sems.at[0, i], recv_sems.at[0, i], across,
        )

    def second(i):
        rows = shards[i].shape[0]
        part = rows // 4
        block = fulls[i].at[pl.ds((1 - y) * rows + (core * 2 + x) * part, part)]
        return remote(block, block, send_sems.at[1, i], recv_sems.at[1, i], beside)

    def third(i):
        rows = shards[i].shape[0]
        part = rows // 2
        block = fulls[i].at[pl.ds((1 - y) * rows + core * part, part)]
        return remote(block, block, send_sems.at[2, i], recv_sems.at[2, i], sibling)

    order = [count - 1] + list(range(count - 1))
    for i in order:
        first(i).start()
    for i in range(count):
        local(i).start()
    first(count - 1).wait_recv()
    big = count - 1
    for step in range(big + 1):
        if step < big:
            first(step).wait_recv()
            second(step).start()
        if step >= 1:
            second(step - 1).wait_recv()
            third(step - 1).start()
    for i in range(big):
        third(i).wait_recv()
    for i in range(count):
        local(i).wait()
        first(i).wait_send()
    for i in range(big):
        second(i).wait_send()
        third(i).wait_send()


def gather_weights(shards):
    count = len(shards)
    return pl.pallas_call(
        functools.partial(gather_kernel, count),
        out_shape=[jax.ShapeDtypeStruct((2 * s.shape[0],) + s.shape[1:], s.dtype) for s in shards],
        in_specs=[pl.BlockSpec(memory_space=pl.ANY)] * count,
        out_specs=[pl.BlockSpec(memory_space=pltpu.VMEM)] * count,
        scratch_shapes=[
            pltpu.SemaphoreType.DMA((count,)),
            pltpu.SemaphoreType.DMA((3, count)),
            pltpu.SemaphoreType.DMA((3, count)),
        ],
        compiler_params=pltpu.CompilerParams(
            collective_id=1, has_side_effects=True, vmem_limit_bytes=48 * 2**20
        ),
        name="gather_weights",
    )(*shards)


def term_groups(lefts, rights, depth):
    groups = []
    for left, right in zip(lefts, rights):
        columns = right.shape[1]
        by_columns = columns % (depth * LANES) == 0
        piece = lefts[0].shape[1] // 8 * LANES
        if by_columns:
            chunks = columns // (depth * LANES)
        else:
            chunks = left.shape[1] * columns // (8 * depth * piece)
        groups.append((left, right, by_columns, chunks))
    return groups


def reduce_kernel(
    count, *refs
):
    reduce_body(refs[:count], refs[count : 2 * count], *refs[2 * count :])


def token_dot(left, right):
    return lax.dot_general(
        left, right, (((0,), (0,)), ((), ())), preferred_element_type=jnp.float32
    ).astype(jnp.bfloat16)


def reduce_body(
    lefts, rights, gains, out, gains_out,
    terms, from_core, from_across, from_beside, from_line, gain_in,
    send_core, recv_core, send_across, recv_across, send_beside, recv_beside,
    send_line, recv_line, send_zline, recv_zline, send_xback, recv_xback,
    send_back, recv_back, send_gain, recv_gain,
):
    chunks = terms.shape[0]
    depth = terms.shape[4]
    x, core, z, y = coordinates()
    sibling = device(x, 1 - core, z, y)
    beside = device(1 - x, core, z, y)
    across = device(x, core, z, 1 - y)
    line = [device(x, core, lax.rem(z + d, depth), y) for d in range(1, depth)]
    greet([sibling, beside, across] + line)

    def to_core(c):
        return remote(terms.at[c, 1 - core], from_core.at[c], send_core.at[c], recv_core.at[c], sibling)

    def to_across(c):
        return remote(
            from_core.at[c, 1 - y], from_across.at[c], send_across.at[c], recv_across.at[c], across
        )

    def to_beside(c):
        return remote(
            from_across.at[c, 1 - x], from_beside.at[c], send_beside.at[c], recv_beside.at[c], beside
        )

    def to_line(c, d):
        return remote(
            from_beside.at[c, lax.rem(z + d, depth)], from_line.at[c, d - 1],
            send_line.at[c, d - 1], recv_line.at[c, d - 1], line[d - 1],
        )

    def along_line(c, d):
        block = out.at[c, core, x, z]
        return remote(block, block, send_zline.at[c, d - 1], recv_zline.at[c, d - 1], line[d - 1])

    def along_line_arrival(c, d):
        block = out.at[c, core, x, lax.rem(z + depth - d, depth)]
        return remote(block, block, send_zline.at[c, d - 1], recv_zline.at[c, d - 1], line[d - 1])

    def back_beside(c, side):
        block = out.at[c, core, side]
        return remote(block, block, send_xback.at[c], recv_xback.at[c], beside)

    def back_core(c, side):
        block = out.at[c, side]
        return remote(block, block, send_back.at[c], recv_back.at[c], sibling)

    def gain_copy(step):
        target = ([sibling, across, beside] + line)[step]
        src = gains if step == 0 else gains_out.at[min(step, 3) - 1]
        return remote(src, gain_in.at[step], send_gain.at[step], recv_gain.at[step], target)

    def add(a, b):
        return (a.astype(jnp.float32) + b.astype(jnp.float32)).astype(jnp.bfloat16)

    gain_copy(0).start()
    piece_rows = terms.shape[5]

    def make_columns(left, right, at, c):
        width = depth * LANES
        block = token_dot(left[...], right[:, pl.ds(pl.multiple_of(at * width, width), width)])
        for side in range(2):
            for own in range(2):
                for across_x in range(2):
                    low = ((side * 2 + own) * 2 + across_x) * piece_rows
                    for place in range(depth):
                        terms[c, own, side, across_x, place] = block[
                            low : low + piece_rows, place * LANES : (place + 1) * LANES
                        ]

    def make_rows(left, right, at, c, parts):
        rows, tiles = left.shape[1] // (2 * parts), right.shape[1] // LANES
        high = rows // (4 * depth)
        for side in range(2):
            start = pl.multiple_of((side * parts + at) * rows, rows)
            block = token_dot(left[:, pl.ds(start, rows)], right[...])
            for own in range(2):
                for across_x in range(2):
                    for place in range(depth):
                        low = ((own * 2 + across_x) * depth + place) * high
                        for tile in range(tiles):
                            terms[
                                c, own, side, across_x, place, tile * high : (tile + 1) * high
                            ] = block[low : low + high, tile * LANES : (tile + 1) * LANES]

    def make(t):
        start = 0
        for left, right, by_columns, parts in term_groups(lefts, rights, depth):
            @pl.when((t >= start) & (t < start + parts))
            def _(left=left, right=right, by_columns=by_columns, parts=parts, start=start):
                if by_columns:
                    make_columns(left, right, t - start, t)
                else:
                    make_rows(left, right, t - start, t, parts)
            start += parts
        to_core(t).start()

    def stage(at, action):
        @pl.when((at >= 0) & (at < chunks))
        def _():
            action(at)

    def after_core(c):
        to_core(c).wait_recv()
        from_core[c, 1 - y] = add(from_core[c, 1 - y], terms[c, core, 1 - y])
        to_across(c).start()
        from_core[c, y] = add(from_core[c, y], terms[c, core, y])

    def after_across(c):
        to_across(c).wait_recv()
        from_across[c, 1 - x] = add(from_across[c, 1 - x], from_core[c, y, 1 - x])
        to_beside(c).start()
        from_across[c, x] = add(from_across[c, x], from_core[c, y, x])

    def after_beside(c):
        to_beside(c).wait_recv()
        from_beside[c] = add(from_beside[c], from_across[c, x])
        for d in range(1, depth):
            to_line(c, d).start()

    def after_line(c):
        total = from_beside[c, z].astype(jnp.float32)
        for d in range(1, depth):
            to_line(c, d).wait_recv()
            total = total + from_line[c, d - 1].astype(jnp.float32)
        out[c, core, x, z] = total.astype(jnp.bfloat16)
        for d in range(1, depth):
            along_line(c, d).start()

    def after_zline(c):
        for d in range(1, depth):
            along_line_arrival(c, d).wait_recv()
        back_beside(c, x).start()

    def after_xback(c):
        back_beside(c, 1 - x).wait_recv()
        back_core(c, core).start()

    actions = [make, after_core, after_across, after_beside, after_line, after_zline, after_xback]

    @pl.loop(0, chunks + len(actions) - 1)
    def _(t):
        for lag, action in enumerate(actions):
            stage(t - lag, action)
        for step in range(3):
            @pl.when(t == step + 1)
            def _():
                gain_copy(step).wait_recv()
                before = gains[...] if step == 0 else gains_out[step - 1]
                gains_out[step] = before + gain_in[step]
                if step < 2:
                    gain_copy(step + 1).start()
                else:
                    for d in range(1, depth):
                        gain_copy(2 + d).start()

    total = gains_out[2]
    for d in range(1, depth):
        gain_copy(2 + d).wait_recv()
        total = total + gain_in[2 + d]
    gains_out[3] = total
    for step in range(2 + depth):
        gain_copy(step).wait_send()

    @pl.loop(0, chunks)
    def _(c):
        back_core(c, 1 - core).wait_recv()
        to_core(c).wait_send()
        to_across(c).wait_send()
        to_beside(c).wait_send()
        for d in range(1, depth):
            to_line(c, d).wait_send()
            along_line(c, d).wait_send()
        back_beside(c, x).wait_send()
        back_core(c, core).wait_send()


def reduce_terms(lefts, rights, gains):
    depth = lax.axis_size("seq") // 4
    groups = term_groups(lefts, rights, depth)
    chunks = sum(group[3] for group in groups)
    piece = (lefts[0].shape[1] // 8, LANES)
    dma = pltpu.SemaphoreType.DMA
    vmem = pl.BlockSpec(memory_space=pltpu.VMEM)
    pair = [dma((chunks,)), dma((chunks,))]
    lines = [dma((chunks, depth - 1)), dma((chunks, depth - 1))]
    steps = 2 + depth
    return pl.pallas_call(
        functools.partial(reduce_kernel, len(lefts)),
        out_shape=[
            jax.ShapeDtypeStruct((chunks, 2, 2, depth) + piece, jnp.bfloat16),
            jax.ShapeDtypeStruct((4,) + gains.shape, jnp.float32),
        ],
        in_specs=[vmem] * (2 * len(lefts) + 1),
        out_specs=[vmem, vmem],
        scratch_shapes=[
            pltpu.VMEM((chunks, 2, 2, 2, depth) + piece, jnp.bfloat16),
            pltpu.VMEM((chunks, 2, 2, depth) + piece, jnp.bfloat16),
            pltpu.VMEM((chunks, 2, depth) + piece, jnp.bfloat16),
            pltpu.VMEM((chunks, depth) + piece, jnp.bfloat16),
            pltpu.VMEM((chunks, depth - 1) + piece, jnp.bfloat16),
            pltpu.VMEM((steps,) + gains.shape, jnp.float32),
        ]
        + pair + pair + pair + lines + lines + pair + pair
        + [dma((steps,)), dma((steps,))],
        compiler_params=pltpu.CompilerParams(
            collective_id=2, has_side_effects=True, vmem_limit_bytes=56 * 2**20
        ),
        name="reduce_terms",
    )(*lefts, *rights, gains)


def unpack_kernel(plan, summed, *outs):
    c = pl.program_id(0)
    depth, rows = summed.shape[3], summed.shape[4]
    for outputs, by_columns, start, parts in plan:
        @pl.when((c >= start) & (c < start + parts))
        def _(outputs=outputs, by_columns=by_columns):
            for core in range(2):
                for x in range(2):
                    for z in range(depth):
                        piece = summed[0, core, x, z].astype(jnp.float32)
                        if by_columns:
                            low = (core * 2 + x) * rows
                            ref, column = outputs[0], z * LANES
                            width = outs[ref].shape[1]
                            ref, column = ref + column // width, column % width
                            outs[ref][low : low + rows, column : column + LANES] = piece
                        else:
                            ref = outs[outputs[0]]
                            tiles = ref.shape[1] // LANES
                            high = rows // tiles
                            low = ((core * 2 + x) * depth + z) * high
                            for tile in range(tiles):
                                ref[low : low + high, tile * LANES : (tile + 1) * LANES] = piece[
                                    tile * high : (tile + 1) * high
                                ]


def unpack(summed, shapes):
    chunks, _, _, depth, rows, lanes = summed.shape
    width = depth * lanes
    plan, shaped, specs, start, index = [], [], [], 0, 0
    while index < len(shapes):
        high, wide = shapes[index]
        together = max(1, width // wide) if wide <= width and width % wide == 0 else 1
        by_columns = (wide * together) % width == 0
        if by_columns:
            parts = wide * together // width
            block = (high, min(wide, width))
        else:
            parts = high * wide // (4 * depth * rows * lanes)
            block = (high // parts, wide)
        plan.append((list(range(index, index + together)), by_columns, start, parts))

        def place(c, start=start, parts=parts, by_columns=by_columns):
            at = jnp.clip(c - start, 0, parts - 1)
            return (0, at) if by_columns else (at, 0)

        for k in range(together):
            shaped.append(jax.ShapeDtypeStruct(shapes[index + k], jnp.float32))
            specs.append(pl.BlockSpec(block, place))
        start += parts
        index += together
    return pl.pallas_call(
        functools.partial(unpack_kernel, plan),
        grid=(chunks,),
        out_shape=shaped,
        in_specs=[pl.BlockSpec((1,) + summed.shape[1:], lambda c: (c, 0, 0, 0, 0, 0))],
        out_specs=specs,
        name="unpack",
    )(summed)


def per_device(
    inputs,
    doc_ids,
    w_query,
    w_key,
    w_value,
    w_out,
    w_gate,
    w_up,
    w_down,
    gain_in,
    gain_attn_post,
    gain_ff_pre,
    gain_ff_post,
    gain_query,
    gain_key,
    cotangent,
):
    small = (gain_in, gain_attn_post, gain_ff_pre, gain_ff_post, gain_query, gain_key)
    small_shard = jnp.concatenate(small).astype(jnp.float32).reshape(1, -1, LANES)
    gathered = gather_weights(
        (w_query, w_key, w_value, w_out, w_gate, w_up, w_down, small_shard)
    )
    full_query, full_key, full_value, full_out, full_gate, full_up, full_down = gathered[:7]
    small_full = gathered[7].reshape(2, -1)
    starts = [0]
    for vec in small:
        starts.append(starts[-1] + vec.shape[0])
    in_gain, attn_post_gain, ff_pre_gain, ff_post_gain, query_gain, key_gain = [
        small_full[:, low:high].reshape(-1) for low, high in zip(starts[:-1], starts[1:])
    ]
    row_count = inputs.shape[0]
    head_dim = full_key.shape[1]
    head_count = full_query.shape[1] // head_dim
    score_scale = head_dim ** (-0.5)
    start_row = lax.axis_index(("seq", "wshard")) * row_count
    query_pos = start_row + jnp.arange(row_count, dtype=jnp.int32)
    cos_table, sin_table = rope_tables(query_pos, head_dim)
    x_float = inputs.astype(jnp.float32)
    normed_in = rms_gain(x_float, in_gain).astype(jnp.bfloat16)
    query_raw = jnp.dot(normed_in, full_query, preferred_element_type=jnp.float32).reshape(
        row_count, head_count, head_dim
    )
    key_raw = jnp.dot(normed_in, full_key, preferred_element_type=jnp.float32)[:, None, :]
    values = jnp.dot(normed_in, full_value, preferred_element_type=jnp.float32).astype(jnp.bfloat16)
    queries = norm_rope(query_raw, query_gain, cos_table, sin_table).astype(jnp.bfloat16)
    key_rot = norm_rope(key_raw, key_gain, cos_table, sin_table)[:, 0].astype(jnp.bfloat16)
    sent_rows = min(WINDOW, row_count)
    hop_count = WINDOW // sent_rows
    outgoing = (key_rot, values, doc_ids)
    halo_keys = []
    halo_values = []
    halo_docs = []
    for distance in range(hop_count, 0, -1):
        arrived = from_behind((outgoing[0], outgoing[1], outgoing[2]), ("seq", "wshard"), distance)
        halo_keys.append(arrived[0])
        halo_values.append(arrived[1])
        halo_docs.append(arrived[2])
    all_keys = jnp.concatenate(halo_keys + [key_rot], 0)
    all_values = jnp.concatenate(halo_values + [values], 0)
    all_docs = jnp.concatenate(halo_docs + [doc_ids], 0)
    key_pos = start_row - WINDOW + jnp.arange(WINDOW + row_count, dtype=jnp.int32)
    allowed = window_mask(query_pos, key_pos, doc_ids, all_docs)
    scores = masked_scores(queries, all_keys, allowed, score_scale)
    row_peak = jnp.max(scores, axis=-1, keepdims=True)
    row_total = jnp.sum(
        jnp.where(allowed[None], jnp.exp(scores - row_peak), 0.0), axis=-1, keepdims=True
    )
    log_total = row_peak + jnp.log(row_total)
    soft = jnp.where(allowed[None], jnp.exp(scores - log_total), 0.0).astype(jnp.bfloat16)
    attended = jnp.einsum("hqk,kd->qhd", soft, all_values, preferred_element_type=jnp.float32)
    attended = attended.reshape(row_count, head_count * head_dim).astype(jnp.bfloat16)
    attn_proj = jnp.dot(attended, full_out, preferred_element_type=jnp.float32)
    resid = x_float + rms_gain(attn_proj, attn_post_gain)
    normed_ff = rms_gain(resid, ff_pre_gain).astype(jnp.bfloat16)
    gate_pre = jnp.dot(normed_ff, full_gate, preferred_element_type=jnp.float32)
    up_pre = jnp.dot(normed_ff, full_up, preferred_element_type=jnp.float32)
    hidden = geglu(gate_pre, up_pre).astype(jnp.bfloat16)
    ff_proj = jnp.dot(hidden, full_down, preferred_element_type=jnp.float32)
    layer_out = (resid + rms_gain(ff_proj, ff_post_gain)).astype(jnp.bfloat16)
    grad_top = cotangent.astype(jnp.float32)
    _, pullback = jax.vjp(rms_gain, ff_proj, ff_post_gain)
    grad_ff_proj, grad_gain_ff_post = pullback(grad_top)
    grad_ff_proj = grad_ff_proj.astype(jnp.bfloat16)
    grad_hidden = lax.dot_general(
        grad_ff_proj, full_down, (((1,), (1,)), ((), ())), preferred_element_type=jnp.float32
    )
    _, pullback = jax.vjp(geglu, gate_pre, up_pre)
    grad_gate, grad_up = pullback(grad_hidden)
    grad_gate = grad_gate.astype(jnp.bfloat16)
    grad_up = grad_up.astype(jnp.bfloat16)
    grad_normed_ff = lax.dot_general(
        grad_gate, full_gate, (((1,), (1,)), ((), ())), preferred_element_type=jnp.float32
    )
    grad_normed_ff = grad_normed_ff + lax.dot_general(
        grad_up, full_up, (((1,), (1,)), ((), ())), preferred_element_type=jnp.float32
    )
    _, pullback = jax.vjp(rms_gain, resid, ff_pre_gain)
    grad_resid_part, grad_gain_ff_pre = pullback(grad_normed_ff)
    grad_resid = grad_top + grad_resid_part
    _, pullback = jax.vjp(rms_gain, attn_proj, attn_post_gain)
    grad_attn_proj, grad_gain_attn_post = pullback(grad_resid)
    grad_attn_proj = grad_attn_proj.astype(jnp.bfloat16)
    grad_attended = lax.dot_general(
        grad_attn_proj, full_out, (((1,), (1,)), ((), ())), preferred_element_type=jnp.float32
    ).astype(jnp.bfloat16)
    grad_heads = grad_attended.reshape(row_count, head_count, head_dim)
    again_scores = masked_scores(queries, all_keys, allowed, score_scale)
    probs = jnp.where(allowed[None], jnp.exp(again_scores - log_total), 0.0)
    grad_soft = jnp.einsum(
        "qhd,kd->hqk", grad_heads, all_values, preferred_element_type=jnp.float32
    )
    row_inner = jnp.sum(probs * grad_soft, axis=-1, keepdims=True)
    grad_score = (probs * (grad_soft - row_inner) * score_scale).astype(jnp.bfloat16)
    grad_queries = jnp.einsum(
        "hqk,kd->qhd", grad_score, all_keys, preferred_element_type=jnp.float32
    )
    grad_keys_all = jnp.einsum(
        "hqk,qhd->kd", grad_score, queries, preferred_element_type=jnp.float32
    )
    grad_values_all = jnp.einsum(
        "hqk,qhd->kd", probs.astype(jnp.bfloat16), grad_heads, preferred_element_type=jnp.float32
    )
    back_keys = jnp.zeros((sent_rows, head_dim), jnp.float32)
    back_values = jnp.zeros((sent_rows, head_dim), jnp.float32)
    for piece_index in range(hop_count):
        distance = hop_count - piece_index
        piece_start = piece_index * sent_rows
        arrived = (
            from_behind(
                grad_keys_all[piece_start : piece_start + sent_rows].astype(jnp.bfloat16),
                ("seq", "wshard"),
                -distance,
            ).astype(jnp.float32),
            from_behind(
                grad_values_all[piece_start : piece_start + sent_rows].astype(jnp.bfloat16),
                ("seq", "wshard"),
                -distance,
            ).astype(jnp.float32),
        )
        back_keys = back_keys + arrived[0]
        back_values = back_values + arrived[1]
    own_keys = grad_keys_all[WINDOW:]
    own_values = grad_values_all[WINDOW:]
    split_row = row_count - sent_rows
    grad_keys = jnp.concatenate([own_keys[:split_row], own_keys + back_keys], 0)
    grad_values = jnp.concatenate([own_values[:split_row], own_values + back_values], 0).astype(
        jnp.bfloat16
    )

    def query_path(tensor, gain_vec):
        return norm_rope(tensor, gain_vec, cos_table, sin_table)

    _, pullback = jax.vjp(query_path, query_raw, query_gain)
    grad_query_raw, grad_gain_query = pullback(grad_queries)
    _, pullback = jax.vjp(query_path, key_raw, key_gain)
    grad_key_raw, grad_gain_key = pullback(grad_keys[:, None, :])
    grad_query_raw = grad_query_raw.reshape(row_count, head_count * head_dim).astype(jnp.bfloat16)
    grad_key_raw = grad_key_raw[:, 0].astype(jnp.bfloat16)
    grad_normed_in = lax.dot_general(
        grad_query_raw, full_query, (((1,), (1,)), ((), ())), preferred_element_type=jnp.float32
    )
    grad_normed_in = grad_normed_in + lax.dot_general(
        grad_key_raw, full_key, (((1,), (1,)), ((), ())), preferred_element_type=jnp.float32
    )
    grad_normed_in = grad_normed_in + lax.dot_general(
        grad_values, full_value, (((1,), (1,)), ((), ())), preferred_element_type=jnp.float32
    )
    _, pullback = jax.vjp(rms_gain, x_float, in_gain)
    grad_input_part, grad_gain_in = pullback(grad_normed_in)
    grad_inputs = grad_resid + grad_input_part
    keys_values = jnp.concatenate([grad_key_raw, grad_values], axis=1)
    lefts = (normed_ff, normed_ff, hidden, normed_in, normed_in, attended)
    rights = (grad_gate, grad_up, grad_ff_proj, grad_query_raw, keys_values, grad_attn_proj)
    gain_terms = (
        grad_gain_in, grad_gain_attn_post, grad_gain_ff_pre, grad_gain_ff_post,
        grad_gain_query, grad_gain_key,
    )
    gain_rows = jnp.concatenate(gain_terms).astype(jnp.bfloat16).astype(jnp.float32)
    summed, gain_sums = reduce_terms(lefts, rights, gain_rows.reshape(-1, LANES))
    sum_gate, sum_up, sum_down, sum_query, sum_key, sum_value, sum_out = unpack(
        summed, [w.shape for w in (w_gate, w_up, w_down, w_query, w_key, w_value, w_out)]
    )
    me = lax.axis_index("wshard")
    gain_sums = gain_sums[3].reshape(-1)
    gain_outs = []
    start = 0
    for term in gain_terms:
        half = term.shape[0] // 2
        gain_outs.append(lax.dynamic_slice_in_dim(gain_sums, start + me * half, half))
        start += term.shape[0]
    return (
        layer_out, grad_inputs, sum_query, sum_key, sum_value, sum_out, sum_gate, sum_up, sum_down,
    ) + tuple(gain_outs)


def per_device_general(
    inputs,
    doc_ids,
    w_query,
    w_key,
    w_value,
    w_out,
    w_gate,
    w_up,
    w_down,
    gain_in,
    gain_attn_post,
    gain_ff_pre,
    gain_ff_post,
    gain_query,
    gain_key,
    cotangent,
):
    gathered = (
        lax.all_gather(w_query, "wshard", axis=0, tiled=True),
        lax.all_gather(w_key, "wshard", axis=0, tiled=True),
        lax.all_gather(w_value, "wshard", axis=0, tiled=True),
        lax.all_gather(w_out, "wshard", axis=0, tiled=True),
        lax.all_gather(w_gate, "wshard", axis=0, tiled=True),
        lax.all_gather(w_up, "wshard", axis=0, tiled=True),
        lax.all_gather(w_down, "wshard", axis=0, tiled=True),
        lax.all_gather(gain_in, "wshard", axis=0, tiled=True),
        lax.all_gather(gain_attn_post, "wshard", axis=0, tiled=True),
        lax.all_gather(gain_ff_pre, "wshard", axis=0, tiled=True),
        lax.all_gather(gain_ff_post, "wshard", axis=0, tiled=True),
        lax.all_gather(gain_query, "wshard", axis=0, tiled=True),
        lax.all_gather(gain_key, "wshard", axis=0, tiled=True),
    )
    full_query, full_key, full_value, full_out, full_gate, full_up, full_down = gathered[:7]
    in_gain, attn_post_gain, ff_pre_gain, ff_post_gain, query_gain, key_gain = [
        g.astype(jnp.float32) for g in gathered[7:]
    ]
    row_count = inputs.shape[0]
    head_dim = full_key.shape[1]
    head_count = full_query.shape[1] // head_dim
    score_scale = head_dim ** (-0.5)
    start_row = lax.axis_index(("seq", "wshard")) * row_count
    query_pos = start_row + jnp.arange(row_count, dtype=jnp.int32)
    cos_table, sin_table = rope_tables(query_pos, head_dim)
    x_float = inputs.astype(jnp.float32)
    normed_in = rms_gain(x_float, in_gain).astype(jnp.bfloat16)
    query_raw = jnp.dot(normed_in, full_query, preferred_element_type=jnp.float32).reshape(
        row_count, head_count, head_dim
    )
    key_raw = jnp.dot(normed_in, full_key, preferred_element_type=jnp.float32)[:, None, :]
    values = jnp.dot(normed_in, full_value, preferred_element_type=jnp.float32).astype(jnp.bfloat16)
    queries = norm_rope(query_raw, query_gain, cos_table, sin_table).astype(jnp.bfloat16)
    key_rot = norm_rope(key_raw, key_gain, cos_table, sin_table)[:, 0].astype(jnp.bfloat16)
    sent_rows = min(WINDOW, row_count)
    hop_count = WINDOW // sent_rows
    outgoing = (key_rot, values, doc_ids)
    halo_keys = []
    halo_values = []
    halo_docs = []
    for distance in range(hop_count, 0, -1):
        arrived = from_behind((outgoing[0], outgoing[1], outgoing[2]), ("seq", "wshard"), distance)
        halo_keys.append(arrived[0])
        halo_values.append(arrived[1])
        halo_docs.append(arrived[2])
    all_keys = jnp.concatenate(halo_keys + [key_rot], 0)
    all_values = jnp.concatenate(halo_values + [values], 0)
    all_docs = jnp.concatenate(halo_docs + [doc_ids], 0)
    key_pos = start_row - WINDOW + jnp.arange(WINDOW + row_count, dtype=jnp.int32)
    allowed = window_mask(query_pos, key_pos, doc_ids, all_docs)
    scores = masked_scores(queries, all_keys, allowed, score_scale)
    row_peak = jnp.max(scores, axis=-1, keepdims=True)
    row_total = jnp.sum(
        jnp.where(allowed[None], jnp.exp(scores - row_peak), 0.0), axis=-1, keepdims=True
    )
    log_total = row_peak + jnp.log(row_total)
    soft = jnp.where(allowed[None], jnp.exp(scores - log_total), 0.0).astype(jnp.bfloat16)
    attended = jnp.einsum("hqk,kd->qhd", soft, all_values, preferred_element_type=jnp.float32)
    attended = attended.reshape(row_count, head_count * head_dim).astype(jnp.bfloat16)
    attn_proj = jnp.dot(attended, full_out, preferred_element_type=jnp.float32)
    resid = x_float + rms_gain(attn_proj, attn_post_gain)
    normed_ff = rms_gain(resid, ff_pre_gain).astype(jnp.bfloat16)
    gate_pre = jnp.dot(normed_ff, full_gate, preferred_element_type=jnp.float32)
    up_pre = jnp.dot(normed_ff, full_up, preferred_element_type=jnp.float32)
    hidden = geglu(gate_pre, up_pre).astype(jnp.bfloat16)
    ff_proj = jnp.dot(hidden, full_down, preferred_element_type=jnp.float32)
    layer_out = (resid + rms_gain(ff_proj, ff_post_gain)).astype(jnp.bfloat16)
    grad_top = cotangent.astype(jnp.float32)
    _, pullback = jax.vjp(rms_gain, ff_proj, ff_post_gain)
    grad_ff_proj, grad_gain_ff_post = pullback(grad_top)
    grad_ff_proj = grad_ff_proj.astype(jnp.bfloat16)
    grad_w_down = weight_grad(hidden, grad_ff_proj)
    grad_hidden = lax.dot_general(
        grad_ff_proj, full_down, (((1,), (1,)), ((), ())), preferred_element_type=jnp.float32
    )
    _, pullback = jax.vjp(geglu, gate_pre, up_pre)
    grad_gate, grad_up = pullback(grad_hidden)
    grad_gate = grad_gate.astype(jnp.bfloat16)
    grad_up = grad_up.astype(jnp.bfloat16)
    grad_w_gate = weight_grad(normed_ff, grad_gate)
    grad_w_up = weight_grad(normed_ff, grad_up)
    grad_normed_ff = lax.dot_general(
        grad_gate, full_gate, (((1,), (1,)), ((), ())), preferred_element_type=jnp.float32
    )
    grad_normed_ff = grad_normed_ff + lax.dot_general(
        grad_up, full_up, (((1,), (1,)), ((), ())), preferred_element_type=jnp.float32
    )
    _, pullback = jax.vjp(rms_gain, resid, ff_pre_gain)
    grad_resid_part, grad_gain_ff_pre = pullback(grad_normed_ff)
    grad_resid = grad_top + grad_resid_part
    ff_gradients = (grad_w_gate, grad_w_up, grad_w_down, grad_gain_ff_pre, grad_gain_ff_post)
    ff_parts = (
        lax.psum_scatter(
            ff_gradients[0].astype(jnp.bfloat16), "wshard", scatter_dimension=0, tiled=True
        ).astype(jnp.float32),
        lax.psum_scatter(
            ff_gradients[1].astype(jnp.bfloat16), "wshard", scatter_dimension=0, tiled=True
        ).astype(jnp.float32),
        lax.psum_scatter(
            ff_gradients[2].astype(jnp.bfloat16), "wshard", scatter_dimension=0, tiled=True
        ).astype(jnp.float32),
        lax.psum_scatter(
            ff_gradients[3].astype(jnp.bfloat16), "wshard", scatter_dimension=0, tiled=True
        ).astype(jnp.float32),
        lax.psum_scatter(
            ff_gradients[4].astype(jnp.bfloat16), "wshard", scatter_dimension=0, tiled=True
        ).astype(jnp.float32),
    )
    ff_reduced = (
        lax.psum(ff_parts[0].astype(jnp.bfloat16), "seq").astype(jnp.float32),
        lax.psum(ff_parts[1].astype(jnp.bfloat16), "seq").astype(jnp.float32),
        lax.psum(ff_parts[2].astype(jnp.bfloat16), "seq").astype(jnp.float32),
        lax.psum(ff_parts[3].astype(jnp.bfloat16), "seq").astype(jnp.float32),
        lax.psum(ff_parts[4].astype(jnp.bfloat16), "seq").astype(jnp.float32),
    )
    _, pullback = jax.vjp(rms_gain, attn_proj, attn_post_gain)
    grad_attn_proj, grad_gain_attn_post = pullback(grad_resid)
    grad_attn_proj = grad_attn_proj.astype(jnp.bfloat16)
    grad_w_out = weight_grad(attended, grad_attn_proj)
    grad_attended = lax.dot_general(
        grad_attn_proj, full_out, (((1,), (1,)), ((), ())), preferred_element_type=jnp.float32
    ).astype(jnp.bfloat16)
    grad_heads = grad_attended.reshape(row_count, head_count, head_dim)
    again_scores = masked_scores(queries, all_keys, allowed, score_scale)
    probs = jnp.where(allowed[None], jnp.exp(again_scores - log_total), 0.0)
    grad_soft = jnp.einsum(
        "qhd,kd->hqk", grad_heads, all_values, preferred_element_type=jnp.float32
    )
    row_inner = jnp.sum(probs * grad_soft, axis=-1, keepdims=True)
    grad_score = (probs * (grad_soft - row_inner) * score_scale).astype(jnp.bfloat16)
    grad_queries = jnp.einsum(
        "hqk,kd->qhd", grad_score, all_keys, preferred_element_type=jnp.float32
    )
    grad_keys_all = jnp.einsum(
        "hqk,qhd->kd", grad_score, queries, preferred_element_type=jnp.float32
    )
    grad_values_all = jnp.einsum(
        "hqk,qhd->kd", probs.astype(jnp.bfloat16), grad_heads, preferred_element_type=jnp.float32
    )
    back_keys = jnp.zeros((sent_rows, head_dim), jnp.float32)
    back_values = jnp.zeros((sent_rows, head_dim), jnp.float32)
    for piece_index in range(hop_count):
        distance = hop_count - piece_index
        piece_start = piece_index * sent_rows
        arrived = (
            from_behind(
                grad_keys_all[piece_start : piece_start + sent_rows].astype(jnp.bfloat16),
                ("seq", "wshard"),
                -distance,
            ).astype(jnp.float32),
            from_behind(
                grad_values_all[piece_start : piece_start + sent_rows].astype(jnp.bfloat16),
                ("seq", "wshard"),
                -distance,
            ).astype(jnp.float32),
        )
        back_keys = back_keys + arrived[0]
        back_values = back_values + arrived[1]
    own_keys = grad_keys_all[WINDOW:]
    own_values = grad_values_all[WINDOW:]
    split_row = row_count - sent_rows
    grad_keys = jnp.concatenate([own_keys[:split_row], own_keys + back_keys], 0)
    grad_values = jnp.concatenate([own_values[:split_row], own_values + back_values], 0).astype(
        jnp.bfloat16
    )

    def query_path(tensor, gain_vec):
        return norm_rope(tensor, gain_vec, cos_table, sin_table)

    _, pullback = jax.vjp(query_path, query_raw, query_gain)
    grad_query_raw, grad_gain_query = pullback(grad_queries)
    _, pullback = jax.vjp(query_path, key_raw, key_gain)
    grad_key_raw, grad_gain_key = pullback(grad_keys[:, None, :])
    grad_query_raw = grad_query_raw.reshape(row_count, head_count * head_dim).astype(jnp.bfloat16)
    grad_key_raw = grad_key_raw[:, 0].astype(jnp.bfloat16)
    grad_w_query = weight_grad(normed_in, grad_query_raw)
    grad_w_key = weight_grad(normed_in, grad_key_raw)
    grad_w_value = weight_grad(normed_in, grad_values)
    grad_normed_in = lax.dot_general(
        grad_query_raw, full_query, (((1,), (1,)), ((), ())), preferred_element_type=jnp.float32
    )
    grad_normed_in = grad_normed_in + lax.dot_general(
        grad_key_raw, full_key, (((1,), (1,)), ((), ())), preferred_element_type=jnp.float32
    )
    grad_normed_in = grad_normed_in + lax.dot_general(
        grad_values, full_value, (((1,), (1,)), ((), ())), preferred_element_type=jnp.float32
    )
    _, pullback = jax.vjp(rms_gain, x_float, in_gain)
    grad_input_part, grad_gain_in = pullback(grad_normed_in)
    grad_inputs = grad_resid + grad_input_part
    attn_gradients = (
        grad_w_query,
        grad_w_key,
        grad_w_value,
        grad_w_out,
        grad_gain_in,
        grad_gain_attn_post,
        grad_gain_query,
        grad_gain_key,
    )
    attn_parts = (
        lax.psum_scatter(
            attn_gradients[0].astype(jnp.bfloat16), "wshard", scatter_dimension=0, tiled=True
        ).astype(jnp.float32),
        lax.psum_scatter(
            attn_gradients[1].astype(jnp.bfloat16), "wshard", scatter_dimension=0, tiled=True
        ).astype(jnp.float32),
        lax.psum_scatter(
            attn_gradients[2].astype(jnp.bfloat16), "wshard", scatter_dimension=0, tiled=True
        ).astype(jnp.float32),
        lax.psum_scatter(
            attn_gradients[3].astype(jnp.bfloat16), "wshard", scatter_dimension=0, tiled=True
        ).astype(jnp.float32),
        lax.psum_scatter(
            attn_gradients[4].astype(jnp.bfloat16), "wshard", scatter_dimension=0, tiled=True
        ).astype(jnp.float32),
        lax.psum_scatter(
            attn_gradients[5].astype(jnp.bfloat16), "wshard", scatter_dimension=0, tiled=True
        ).astype(jnp.float32),
        lax.psum_scatter(
            attn_gradients[6].astype(jnp.bfloat16), "wshard", scatter_dimension=0, tiled=True
        ).astype(jnp.float32),
        lax.psum_scatter(
            attn_gradients[7].astype(jnp.bfloat16), "wshard", scatter_dimension=0, tiled=True
        ).astype(jnp.float32),
    )
    attn_reduced = (
        lax.psum(attn_parts[0].astype(jnp.bfloat16), "seq").astype(jnp.float32),
        lax.psum(attn_parts[1].astype(jnp.bfloat16), "seq").astype(jnp.float32),
        lax.psum(attn_parts[2].astype(jnp.bfloat16), "seq").astype(jnp.float32),
        lax.psum(attn_parts[3].astype(jnp.bfloat16), "seq").astype(jnp.float32),
        lax.psum(attn_parts[4].astype(jnp.bfloat16), "seq").astype(jnp.float32),
        lax.psum(attn_parts[5].astype(jnp.bfloat16), "seq").astype(jnp.float32),
        lax.psum(attn_parts[6].astype(jnp.bfloat16), "seq").astype(jnp.float32),
        lax.psum(attn_parts[7].astype(jnp.bfloat16), "seq").astype(jnp.float32),
    )
    reduced = (
        attn_reduced[0],
        attn_reduced[1],
        attn_reduced[2],
        attn_reduced[3],
        ff_reduced[0],
        ff_reduced[1],
        ff_reduced[2],
        attn_reduced[4],
        attn_reduced[5],
        ff_reduced[3],
        ff_reduced[4],
        attn_reduced[6],
        attn_reduced[7],
    )
    return (layer_out, grad_inputs) + tuple(reduced)


def solution(mesh):
    routed = mesh.shape["wshard"] == 2 and mesh.shape["seq"] == 16
    return jax.shard_map(
        per_device if routed else per_device_general,
        mesh=mesh,
        in_specs=(
            P(("seq", "wshard"), None),
            P(("seq", "wshard")),
            P("wshard", None),
            P("wshard", None),
            P("wshard", None),
            P("wshard", None),
            P("wshard", None),
            P("wshard", None),
            P("wshard", None),
            P("wshard"),
            P("wshard"),
            P("wshard"),
            P("wshard"),
            P("wshard"),
            P("wshard"),
            P(("seq", "wshard"), None),
        ),
        out_specs=(
            P(("seq", "wshard"), None),
            P(("seq", "wshard"), None),
            P("wshard", None),
            P("wshard", None),
            P("wshard", None),
            P("wshard", None),
            P("wshard", None),
            P("wshard", None),
            P("wshard", None),
            P("wshard"),
            P("wshard"),
            P("wshard"),
            P("wshard"),
            P("wshard"),
            P("wshard"),
        ),
        check_vma=False,
    )
```

```python
import functools

import jax
import jax.numpy as jnp
from jax import lax
from jax.experimental import pallas as pl
from jax.experimental.pallas import tpu as pltpu
from jax.sharding import PartitionSpec as P

WINDOW = 512


NORM_EPSILON = 1e-06
ROPE_BASE = 10000.0
MASK_FLOOR = -1e30


def from_behind(array, axis, by):
    count = lax.axis_size(axis)
    pairs = [(i, i + by) for i in range(count) if 0 <= i + by < count]
    return lax.ppermute(array, axis, pairs)


def rms_gain(tensor, gain_vec):
    factor = lax.rsqrt(jnp.mean(tensor * tensor, axis=-1, keepdims=True) + NORM_EPSILON)
    return tensor * factor * (1.0 + gain_vec)


def rope_tables(positions, head_width):
    half_width = head_width // 2
    exponent = jnp.arange(half_width, dtype=jnp.float32) * (2.0 / head_width)
    inverse = jnp.exp(-jnp.log(ROPE_BASE) * exponent)
    angles = positions.astype(jnp.float32)[:, None] * inverse[None, :]
    return (jnp.cos(angles), jnp.sin(angles))


def norm_rope(tensor, gain_vec, cos_table, sin_table):
    normed = rms_gain(tensor, gain_vec)
    half_width = tensor.shape[-1] // 2
    front_part = normed[..., :half_width]
    back_part = normed[..., half_width:]
    cos_rows = cos_table[:, None, :]
    sin_rows = sin_table[:, None, :]
    return jnp.concatenate(
        [
            front_part * cos_rows - back_part * sin_rows,
            back_part * cos_rows + front_part * sin_rows,
        ],
        axis=-1,
    )


def geglu(gate_pre, up_pre):
    return jax.nn.gelu(gate_pre, approximate=True) * up_pre


def window_mask(query_pos, key_pos, query_doc, key_doc):
    distance = query_pos[:, None] - key_pos[None, :]
    return (
        (distance >= 0)
        & (distance < WINDOW)
        & (key_pos[None, :] >= 0)
        & (query_doc[:, None] == key_doc[None, :])
    )


def masked_scores(queries, all_keys, allowed, score_scale):
    scores = (
        jnp.einsum("qhd,kd->hqk", queries, all_keys, preferred_element_type=jnp.float32)
        * score_scale
    )
    return jnp.where(allowed[None], scores, MASK_FLOOR)


def weight_grad(left_rows, right_rows):
    return jnp.einsum("tc,tf->cf", left_rows, right_rows, preferred_element_type=jnp.float32)


MESH = pl.DeviceIdType.MESH
LANES = 128


def coordinates():
    seq = lax.axis_index("seq")
    return lax.rem(seq // 2, 2), lax.rem(seq, 2), seq // 4, lax.axis_index("wshard")


def device(x, core, z, y):
    return ((z * 2 + x) * 2 + core, y)


def greet(partners):
    barrier = pltpu.get_barrier_semaphore()
    for partner in partners:
        pl.semaphore_signal(barrier, inc=1, device_id=partner, device_id_type=MESH)
    pl.semaphore_wait(barrier, len(partners))


def remote(src, dst, send, recv, target):
    return pltpu.make_async_remote_copy(
        src_ref=src, dst_ref=dst, send_sem=send, recv_sem=recv,
        device_id=target, device_id_type=MESH,
    )


def gather_kernel(count, *refs):
    shards, fulls = refs[:count], refs[count : 2 * count]
    own_sem, send_sems, recv_sems = refs[2 * count :]
    x, core, z, y = coordinates()
    sibling = device(x, 1 - core, z, y)
    beside = device(1 - x, core, z, y)
    across = device(x, core, z, 1 - y)
    greet([sibling, beside, across])

    def local(i):
        rows = shards[i].shape[0]
        return pltpu.make_async_copy(
            shards[i], fulls[i].at[pl.ds(y * rows, rows)], own_sem.at[i]
        )

    def first(i):
        rows = shards[i].shape[0]
        part = rows if i == count - 1 else rows // 4
        at = 0 if i == count - 1 else (core * 2 + x) * part
        return remote(
            shards[i].at[pl.ds(at, part)], fulls[i].at[pl.ds(y * rows + at, part)],
            send_sems.at[0, i], recv_sems.at[0, i], across,
        )

    def second(i):
        rows = shards[i].shape[0]
        part = rows // 4
        block = fulls[i].at[pl.ds((1 - y) * rows + (core * 2 + x) * part, part)]
        return remote(block, block, send_sems.at[1, i], recv_sems.at[1, i], beside)

    def third(i):
        rows = shards[i].shape[0]
        part = rows // 2
        block = fulls[i].at[pl.ds((1 - y) * rows + core * part, part)]
        return remote(block, block, send_sems.at[2, i], recv_sems.at[2, i], sibling)

    order = [count - 1] + list(range(count - 1))
    for i in order:
        first(i).start()
    for i in range(count):
        local(i).start()
    first(count - 1).wait_recv()
    big = count - 1
    for step in range(big + 1):
        if step < big:
            first(step).wait_recv()
            second(step).start()
        if step >= 1:
            second(step - 1).wait_recv()
            third(step - 1).start()
    for i in range(big):
        third(i).wait_recv()
    for i in range(count):
        local(i).wait()
        first(i).wait_send()
    for i in range(big):
        second(i).wait_send()
        third(i).wait_send()


def gather_weights(shards):
    count = len(shards)
    return pl.pallas_call(
        functools.partial(gather_kernel, count),
        out_shape=[jax.ShapeDtypeStruct((2 * s.shape[0],) + s.shape[1:], s.dtype) for s in shards],
        in_specs=[pl.BlockSpec(memory_space=pl.ANY)] * count,
        out_specs=[pl.BlockSpec(memory_space=pltpu.VMEM)] * count,
        scratch_shapes=[
            pltpu.SemaphoreType.DMA((count,)),
            pltpu.SemaphoreType.DMA((3, count)),
            pltpu.SemaphoreType.DMA((3, count)),
        ],
        compiler_params=pltpu.CompilerParams(
            collective_id=1, has_side_effects=True, vmem_limit_bytes=58 * 2**20
        ),
        name="gather_weights",
    )(*shards)


def term_groups(lefts, rights, depth):
    groups = []
    for left, right in zip(lefts, rights):
        columns = right.shape[1]
        by_columns = columns % (depth * LANES) == 0
        piece = lefts[0].shape[1] // 8 * LANES
        if by_columns:
            chunks = columns // (depth * LANES)
        else:
            chunks = left.shape[1] * columns // (8 * depth * piece)
        groups.append((left, right, by_columns, chunks))
    return groups


def reduce_kernel(
    count, *refs
):
    reduce_body(refs[:count], refs[count : 2 * count], *refs[2 * count :])


def token_dot(left, right):
    return lax.dot_general(
        left, right, (((0,), (0,)), ((), ())), preferred_element_type=jnp.float32
    ).astype(jnp.bfloat16)


def reduce_body(
    lefts, rights, gains, out, gains_out,
    terms, from_core, from_across, from_beside, from_line, gain_in,
    send_core, recv_core, send_across, recv_across, send_beside, recv_beside,
    send_line, recv_line, send_zline, recv_zline, send_xback, recv_xback,
    send_back, recv_back, send_gain, recv_gain,
):
    chunks = terms.shape[0]
    depth = terms.shape[4]
    x, core, z, y = coordinates()
    sibling = device(x, 1 - core, z, y)
    beside = device(1 - x, core, z, y)
    across = device(x, core, z, 1 - y)
    line = [device(x, core, lax.rem(z + d, depth), y) for d in range(1, depth)]
    greet([sibling, beside, across] + line)

    def to_core(c):
        return remote(terms.at[c, 1 - core], from_core.at[c], send_core.at[c], recv_core.at[c], sibling)

    def to_across(c):
        return remote(
            from_core.at[c, 1 - y], from_across.at[c], send_across.at[c], recv_across.at[c], across
        )

    def to_beside(c):
        return remote(
            from_across.at[c, 1 - x], from_beside.at[c], send_beside.at[c], recv_beside.at[c], beside
        )

    def to_line(c, d):
        return remote(
            from_beside.at[c, lax.rem(z + d, depth)], from_line.at[c, d - 1],
            send_line.at[c, d - 1], recv_line.at[c, d - 1], line[d - 1],
        )

    def along_line(c, d):
        block = out.at[c, core, x, z]
        return remote(block, block, send_zline.at[c, d - 1], recv_zline.at[c, d - 1], line[d - 1])

    def along_line_arrival(c, d):
        block = out.at[c, core, x, lax.rem(z + depth - d, depth)]
        return remote(block, block, send_zline.at[c, d - 1], recv_zline.at[c, d - 1], line[d - 1])

    def back_beside(c, side):
        block = out.at[c, core, side]
        return remote(block, block, send_xback.at[c], recv_xback.at[c], beside)

    def back_core(c, side):
        block = out.at[c, side]
        return remote(block, block, send_back.at[c], recv_back.at[c], sibling)

    def gain_copy(step):
        target = ([sibling, across, beside] + line)[step]
        src = gains if step == 0 else gains_out.at[min(step, 3) - 1]
        return remote(src, gain_in.at[step], send_gain.at[step], recv_gain.at[step], target)

    def add(a, b):
        return (a.astype(jnp.float32) + b.astype(jnp.float32)).astype(jnp.bfloat16)

    gain_copy(0).start()
    piece_rows = terms.shape[5]

    def make_columns(left, right, at, c):
        width = depth * LANES
        block = token_dot(left[...], right[:, pl.ds(pl.multiple_of(at * width, width), width)])
        for side in range(2):
            for own in range(2):
                for across_x in range(2):
                    low = ((side * 2 + own) * 2 + across_x) * piece_rows
                    for place in range(depth):
                        terms[c, own, side, across_x, place] = block[
                            low : low + piece_rows, place * LANES : (place + 1) * LANES
                        ]

    def make_rows(left, right, at, c, parts):
        rows, tiles = left.shape[1] // (2 * parts), right.shape[1] // LANES
        high = rows // (4 * depth)
        for side in range(2):
            start = pl.multiple_of((side * parts + at) * rows, rows)
            block = token_dot(left[:, pl.ds(start, rows)], right[...])
            for own in range(2):
                for across_x in range(2):
                    for place in range(depth):
                        low = ((own * 2 + across_x) * depth + place) * high
                        for tile in range(tiles):
                            terms[
                                c, own, side, across_x, place, tile * high : (tile + 1) * high
                            ] = block[low : low + high, tile * LANES : (tile + 1) * LANES]

    def make(t):
        start = 0
        for left, right, by_columns, parts in term_groups(lefts, rights, depth):
            @pl.when((t >= start) & (t < start + parts))
            def _(left=left, right=right, by_columns=by_columns, parts=parts, start=start):
                if by_columns:
                    make_columns(left, right, t - start, t)
                else:
                    make_rows(left, right, t - start, t, parts)
            start += parts
        to_core(t).start()

    def stage(at, action):
        @pl.when((at >= 0) & (at < chunks))
        def _():
            action(at)

    def after_core(c):
        to_core(c).wait_recv()
        from_core[c, 1 - y] = add(from_core[c, 1 - y], terms[c, core, 1 - y])
        to_across(c).start()
        from_core[c, y] = add(from_core[c, y], terms[c, core, y])

    def after_across(c):
        to_across(c).wait_recv()
        from_across[c, 1 - x] = add(from_across[c, 1 - x], from_core[c, y, 1 - x])
        to_beside(c).start()
        from_across[c, x] = add(from_across[c, x], from_core[c, y, x])

    def after_beside(c):
        to_beside(c).wait_recv()
        from_beside[c] = add(from_beside[c], from_across[c, x])
        for d in range(1, depth):
            to_line(c, d).start()

    def after_line(c):
        total = from_beside[c, z].astype(jnp.float32)
        for d in range(1, depth):
            to_line(c, d).wait_recv()
            total = total + from_line[c, d - 1].astype(jnp.float32)
        out[c, core, x, z] = total.astype(jnp.bfloat16)
        for d in range(1, depth):
            along_line(c, d).start()

    def after_zline(c):
        for d in range(1, depth):
            along_line_arrival(c, d).wait_recv()
        back_beside(c, x).start()

    def after_xback(c):
        back_beside(c, 1 - x).wait_recv()
        back_core(c, core).start()

    actions = [make, after_core, after_across, after_beside, after_line, after_zline, after_xback]

    @pl.loop(0, chunks + len(actions) - 1)
    def _(t):
        for lag, action in enumerate(actions):
            stage(t - lag, action)
        for step in range(3):
            @pl.when(t == step + 1)
            def _():
                gain_copy(step).wait_recv()
                before = gains[...] if step == 0 else gains_out[step - 1]
                gains_out[step] = before + gain_in[step]
                if step < 2:
                    gain_copy(step + 1).start()
                else:
                    for d in range(1, depth):
                        gain_copy(2 + d).start()

    total = gains_out[2]
    for d in range(1, depth):
        gain_copy(2 + d).wait_recv()
        total = total + gain_in[2 + d]
    gains_out[3] = total
    for step in range(2 + depth):
        gain_copy(step).wait_send()

    @pl.loop(0, chunks)
    def _(c):
        back_core(c, 1 - core).wait_recv()
        to_core(c).wait_send()
        to_across(c).wait_send()
        to_beside(c).wait_send()
        for d in range(1, depth):
            to_line(c, d).wait_send()
            along_line(c, d).wait_send()
        back_beside(c, x).wait_send()
        back_core(c, core).wait_send()


def reduce_terms(lefts, rights, gains):
    depth = lax.axis_size("seq") // 4
    groups = term_groups(lefts, rights, depth)
    chunks = sum(group[3] for group in groups)
    piece = (lefts[0].shape[1] // 8, LANES)
    dma = pltpu.SemaphoreType.DMA
    vmem = pl.BlockSpec(memory_space=pltpu.VMEM)
    pair = [dma((chunks,)), dma((chunks,))]
    lines = [dma((chunks, depth - 1)), dma((chunks, depth - 1))]
    steps = 2 + depth
    return pl.pallas_call(
        functools.partial(reduce_kernel, len(lefts)),
        out_shape=[
            jax.ShapeDtypeStruct((chunks, 2, 2, depth) + piece, jnp.bfloat16),
            jax.ShapeDtypeStruct((4,) + gains.shape, jnp.float32),
        ],
        in_specs=[vmem] * (2 * len(lefts) + 1),
        out_specs=[vmem, vmem],
        scratch_shapes=[
            pltpu.VMEM((chunks, 2, 2, 2, depth) + piece, jnp.bfloat16),
            pltpu.VMEM((chunks, 2, 2, depth) + piece, jnp.bfloat16),
            pltpu.VMEM((chunks, 2, depth) + piece, jnp.bfloat16),
            pltpu.VMEM((chunks, depth) + piece, jnp.bfloat16),
            pltpu.VMEM((chunks, depth - 1) + piece, jnp.bfloat16),
            pltpu.VMEM((steps,) + gains.shape, jnp.float32),
        ]
        + pair + pair + pair + lines + lines + pair + pair
        + [dma((steps,)), dma((steps,))],
        compiler_params=pltpu.CompilerParams(
            collective_id=2, has_side_effects=True, vmem_limit_bytes=56 * 2**20
        ),
        name="reduce_terms",
    )(*lefts, *rights, gains)


def unpack_kernel(plan, summed, *outs):
    c = pl.program_id(0)
    depth, rows = summed.shape[3], summed.shape[4]
    for outputs, by_columns, start, parts in plan:
        @pl.when((c >= start) & (c < start + parts))
        def _(outputs=outputs, by_columns=by_columns):
            for core in range(2):
                for x in range(2):
                    for z in range(depth):
                        piece = summed[0, core, x, z].astype(jnp.float32)
                        if by_columns:
                            low = (core * 2 + x) * rows
                            ref, column = outputs[0], z * LANES
                            width = outs[ref].shape[1]
                            ref, column = ref + column // width, column % width
                            outs[ref][low : low + rows, column : column + LANES] = piece
                        else:
                            ref = outs[outputs[0]]
                            tiles = ref.shape[1] // LANES
                            high = rows // tiles
                            low = ((core * 2 + x) * depth + z) * high
                            for tile in range(tiles):
                                ref[low : low + high, tile * LANES : (tile + 1) * LANES] = piece[
                                    tile * high : (tile + 1) * high
                                ]


def unpack(summed, shapes):
    chunks, _, _, depth, rows, lanes = summed.shape
    width = depth * lanes
    plan, shaped, specs, start, index = [], [], [], 0, 0
    while index < len(shapes):
        high, wide = shapes[index]
        together = max(1, width // wide) if wide <= width and width % wide == 0 else 1
        by_columns = (wide * together) % width == 0
        if by_columns:
            parts = wide * together // width
            block = (high, min(wide, width))
        else:
            parts = high * wide // (4 * depth * rows * lanes)
            block = (high // parts, wide)
        plan.append((list(range(index, index + together)), by_columns, start, parts))

        def place(c, start=start, parts=parts, by_columns=by_columns):
            at = jnp.clip(c - start, 0, parts - 1)
            return (0, at) if by_columns else (at, 0)

        for k in range(together):
            shaped.append(jax.ShapeDtypeStruct(shapes[index + k], jnp.float32))
            specs.append(pl.BlockSpec(block, place))
        start += parts
        index += together
    return pl.pallas_call(
        functools.partial(unpack_kernel, plan),
        grid=(chunks,),
        out_shape=shaped,
        in_specs=[pl.BlockSpec((1,) + summed.shape[1:], lambda c: (c, 0, 0, 0, 0, 0))],
        out_specs=specs,
        name="unpack",
    )(summed)


def shift_kernel(count, hops, step, *refs):
    arrays, outs = refs[:count], refs[count : 2 * count]
    send_sems, recv_sems = refs[2 * count :]
    width = lax.axis_size("wshard")
    total = lax.axis_size("seq") * width
    me = lax.axis_index("seq") * width + lax.axis_index("wshard")
    barrier = pltpu.get_barrier_semaphore()
    offsets = [d for d in range(-hops, hops + 1) if d != 0]

    def there(offset):
        return (me + offset >= 0) & (me + offset < total)

    def target(offset):
        place = lax.rem(me + offset + total, total)
        return (place // width, lax.rem(place, width))

    for offset in offsets:
        pl.semaphore_signal(
            barrier, inc=1, device_id=target(offset), device_id_type=MESH
        )
    pl.semaphore_wait(barrier, len(offsets))

    def copy(k, d):
        source = arrays[k] if step > 0 else arrays[k].at[hops - d]
        return remote(
            source, outs[k].at[d - 1], send_sems.at[k, d - 1], recv_sems.at[k, d - 1],
            target(step * d),
        )

    for d in range(1, hops + 1):
        @pl.when(there(step * d))
        def _():
            for k in range(count):
                copy(k, d).start()
    for d in range(1, hops + 1):
        @pl.when(there(-step * d))
        def _():
            for k in range(count):
                copy(k, d).wait_recv()

        @pl.when(jnp.logical_not(there(-step * d)))
        def _():
            for k in range(count):
                outs[k][d - 1] = jnp.zeros(outs[k].shape[1:], outs[k].dtype)
    for d in range(1, hops + 1):
        @pl.when(there(step * d))
        def _():
            for k in range(count):
                copy(k, d).wait_send()


def shift(arrays, hops, step, name, collective_id):
    count = len(arrays)
    vmem = pl.BlockSpec(memory_space=pltpu.VMEM)
    shapes = [a.shape if step > 0 else a.shape[1:] for a in arrays]
    return pl.pallas_call(
        functools.partial(shift_kernel, count, hops, step),
        out_shape=[
            jax.ShapeDtypeStruct((hops,) + s, a.dtype) for s, a in zip(shapes, arrays)
        ],
        in_specs=[vmem] * count,
        out_specs=[vmem] * count,
        scratch_shapes=[
            pltpu.SemaphoreType.DMA((count, hops)),
            pltpu.SemaphoreType.DMA((count, hops)),
        ],
        compiler_params=pltpu.CompilerParams(collective_id=collective_id, has_side_effects=True),
        name=name,
    )(*arrays)


def per_device(
    inputs,
    doc_ids,
    w_query,
    w_key,
    w_value,
    w_out,
    w_gate,
    w_up,
    w_down,
    gain_in,
    gain_attn_post,
    gain_ff_pre,
    gain_ff_post,
    gain_query,
    gain_key,
    cotangent,
):
    small = (gain_in, gain_attn_post, gain_ff_pre, gain_ff_post, gain_query, gain_key)
    small_shard = jnp.concatenate(small).astype(jnp.float32).reshape(1, -1, LANES)
    gathered = gather_weights(
        (w_query, w_key, w_value, w_out, w_gate, w_up, w_down, small_shard)
    )
    full_query, full_key, full_value, full_out, full_gate, full_up, full_down = gathered[:7]
    small_full = gathered[7].reshape(2, -1)
    starts = [0]
    for vec in small:
        starts.append(starts[-1] + vec.shape[0])
    in_gain, attn_post_gain, ff_pre_gain, ff_post_gain, query_gain, key_gain = [
        small_full[:, low:high].reshape(-1) for low, high in zip(starts[:-1], starts[1:])
    ]
    row_count = inputs.shape[0]
    head_dim = full_key.shape[1]
    head_count = full_query.shape[1] // head_dim
    score_scale = head_dim ** (-0.5)
    start_row = lax.axis_index(("seq", "wshard")) * row_count
    query_pos = start_row + jnp.arange(row_count, dtype=jnp.int32)
    cos_table, sin_table = rope_tables(query_pos, head_dim)
    x_float = inputs.astype(jnp.float32)
    normed_in = rms_gain(x_float, in_gain).astype(jnp.bfloat16)
    query_raw = jnp.dot(normed_in, full_query, preferred_element_type=jnp.float32).reshape(
        row_count, head_count, head_dim
    )
    key_raw = jnp.dot(normed_in, full_key, preferred_element_type=jnp.float32)[:, None, :]
    values = jnp.dot(normed_in, full_value, preferred_element_type=jnp.float32).astype(jnp.bfloat16)
    queries = norm_rope(query_raw, query_gain, cos_table, sin_table).astype(jnp.bfloat16)
    key_rot = norm_rope(key_raw, key_gain, cos_table, sin_table)[:, 0].astype(jnp.bfloat16)
    sent_rows = min(WINDOW, row_count)
    hop_count = WINDOW // sent_rows
    arrived = shift(
        (key_rot, values, doc_ids.reshape(-1, LANES)), hop_count, 1, "shift_on", 3
    )
    order = range(hop_count - 1, -1, -1)
    halo_keys = [arrived[0][i] for i in order]
    halo_values = [arrived[1][i] for i in order]
    halo_docs = [arrived[2][i].reshape(-1) for i in order]
    all_keys = jnp.concatenate(halo_keys + [key_rot], 0)
    all_values = jnp.concatenate(halo_values + [values], 0)
    all_docs = jnp.concatenate(halo_docs + [doc_ids], 0)
    key_pos = start_row - WINDOW + jnp.arange(WINDOW + row_count, dtype=jnp.int32)
    allowed = window_mask(query_pos, key_pos, doc_ids, all_docs)
    scores = masked_scores(queries, all_keys, allowed, score_scale)
    row_peak = jnp.max(scores, axis=-1, keepdims=True)
    row_total = jnp.sum(
        jnp.where(allowed[None], jnp.exp(scores - row_peak), 0.0), axis=-1, keepdims=True
    )
    log_total = row_peak + jnp.log(row_total)
    soft = jnp.where(allowed[None], jnp.exp(scores - log_total), 0.0).astype(jnp.bfloat16)
    attended = jnp.einsum("hqk,kd->qhd", soft, all_values, preferred_element_type=jnp.float32)
    attended = attended.reshape(row_count, head_count * head_dim).astype(jnp.bfloat16)
    attn_proj = jnp.dot(attended, full_out, preferred_element_type=jnp.float32)
    resid = x_float + rms_gain(attn_proj, attn_post_gain)
    normed_ff = rms_gain(resid, ff_pre_gain).astype(jnp.bfloat16)
    gate_pre = jnp.dot(normed_ff, full_gate, preferred_element_type=jnp.float32)
    up_pre = jnp.dot(normed_ff, full_up, preferred_element_type=jnp.float32)
    hidden = geglu(gate_pre, up_pre).astype(jnp.bfloat16)
    ff_proj = jnp.dot(hidden, full_down, preferred_element_type=jnp.float32)
    layer_out = (resid + rms_gain(ff_proj, ff_post_gain)).astype(jnp.bfloat16)
    grad_top = cotangent.astype(jnp.float32)
    _, pullback = jax.vjp(rms_gain, ff_proj, ff_post_gain)
    grad_ff_proj, grad_gain_ff_post = pullback(grad_top)
    grad_ff_proj = grad_ff_proj.astype(jnp.bfloat16)
    grad_hidden = lax.dot_general(
        grad_ff_proj, full_down, (((1,), (1,)), ((), ())), preferred_element_type=jnp.float32
    )
    _, pullback = jax.vjp(geglu, gate_pre, up_pre)
    grad_gate, grad_up = pullback(grad_hidden)
    grad_gate = grad_gate.astype(jnp.bfloat16)
    grad_up = grad_up.astype(jnp.bfloat16)
    grad_normed_ff = lax.dot_general(
        grad_gate, full_gate, (((1,), (1,)), ((), ())), preferred_element_type=jnp.float32
    )
    grad_normed_ff = grad_normed_ff + lax.dot_general(
        grad_up, full_up, (((1,), (1,)), ((), ())), preferred_element_type=jnp.float32
    )
    _, pullback = jax.vjp(rms_gain, resid, ff_pre_gain)
    grad_resid_part, grad_gain_ff_pre = pullback(grad_normed_ff)
    grad_resid = grad_top + grad_resid_part
    _, pullback = jax.vjp(rms_gain, attn_proj, attn_post_gain)
    grad_attn_proj, grad_gain_attn_post = pullback(grad_resid)
    grad_attn_proj = grad_attn_proj.astype(jnp.bfloat16)
    grad_attended = lax.dot_general(
        grad_attn_proj, full_out, (((1,), (1,)), ((), ())), preferred_element_type=jnp.float32
    ).astype(jnp.bfloat16)
    grad_heads = grad_attended.reshape(row_count, head_count, head_dim)
    again_scores = masked_scores(queries, all_keys, allowed, score_scale)
    probs = jnp.where(allowed[None], jnp.exp(again_scores - log_total), 0.0)
    grad_soft = jnp.einsum(
        "qhd,kd->hqk", grad_heads, all_values, preferred_element_type=jnp.float32
    )
    row_inner = jnp.sum(probs * grad_soft, axis=-1, keepdims=True)
    grad_score = (probs * (grad_soft - row_inner) * score_scale).astype(jnp.bfloat16)
    grad_queries = jnp.einsum(
        "hqk,kd->qhd", grad_score, all_keys, preferred_element_type=jnp.float32
    )
    grad_keys_all = jnp.einsum(
        "hqk,qhd->kd", grad_score, queries, preferred_element_type=jnp.float32
    )
    grad_values_all = jnp.einsum(
        "hqk,qhd->kd", probs.astype(jnp.bfloat16), grad_heads, preferred_element_type=jnp.float32
    )
    pieces = (hop_count, sent_rows, head_dim)
    returned = shift(
        (
            grad_keys_all[:WINDOW].astype(jnp.bfloat16).reshape(pieces),
            grad_values_all[:WINDOW].astype(jnp.bfloat16).reshape(pieces),
        ),
        hop_count, -1, "shift_back", 4,
    )
    back_keys, back_values = [jnp.sum(r.astype(jnp.float32), axis=0) for r in returned]
    own_keys = grad_keys_all[WINDOW:]
    own_values = grad_values_all[WINDOW:]
    split_row = row_count - sent_rows
    grad_keys = jnp.concatenate([own_keys[:split_row], own_keys + back_keys], 0)
    grad_values = jnp.concatenate([own_values[:split_row], own_values + back_values], 0).astype(
        jnp.bfloat16
    )

    def query_path(tensor, gain_vec):
        return norm_rope(tensor, gain_vec, cos_table, sin_table)

    _, pullback = jax.vjp(query_path, query_raw, query_gain)
    grad_query_raw, grad_gain_query = pullback(grad_queries)
    _, pullback = jax.vjp(query_path, key_raw, key_gain)
    grad_key_raw, grad_gain_key = pullback(grad_keys[:, None, :])
    grad_query_raw = grad_query_raw.reshape(row_count, head_count * head_dim).astype(jnp.bfloat16)
    grad_key_raw = grad_key_raw[:, 0].astype(jnp.bfloat16)
    grad_normed_in = lax.dot_general(
        grad_query_raw, full_query, (((1,), (1,)), ((), ())), preferred_element_type=jnp.float32
    )
    grad_normed_in = grad_normed_in + lax.dot_general(
        grad_key_raw, full_key, (((1,), (1,)), ((), ())), preferred_element_type=jnp.float32
    )
    grad_normed_in = grad_normed_in + lax.dot_general(
        grad_values, full_value, (((1,), (1,)), ((), ())), preferred_element_type=jnp.float32
    )
    _, pullback = jax.vjp(rms_gain, x_float, in_gain)
    grad_input_part, grad_gain_in = pullback(grad_normed_in)
    grad_inputs = grad_resid + grad_input_part
    keys_values = jnp.concatenate([grad_key_raw, grad_values], axis=1)
    lefts = (normed_ff, normed_ff, hidden, normed_in, normed_in, attended)
    rights = (grad_gate, grad_up, grad_ff_proj, grad_query_raw, keys_values, grad_attn_proj)
    gain_terms = (
        grad_gain_in, grad_gain_attn_post, grad_gain_ff_pre, grad_gain_ff_post,
        grad_gain_query, grad_gain_key,
    )
    gain_rows = jnp.concatenate(gain_terms).astype(jnp.bfloat16).astype(jnp.float32)
    summed, gain_sums = reduce_terms(lefts, rights, gain_rows.reshape(-1, LANES))
    sum_gate, sum_up, sum_down, sum_query, sum_key, sum_value, sum_out = unpack(
        summed, [w.shape for w in (w_gate, w_up, w_down, w_query, w_key, w_value, w_out)]
    )
    me = lax.axis_index("wshard")
    gain_sums = gain_sums[3].reshape(-1)
    gain_outs = []
    start = 0
    for term in gain_terms:
        half = term.shape[0] // 2
        gain_outs.append(lax.dynamic_slice_in_dim(gain_sums, start + me * half, half))
        start += term.shape[0]
    return (
        layer_out, grad_inputs, sum_query, sum_key, sum_value, sum_out, sum_gate, sum_up, sum_down,
    ) + tuple(gain_outs)


def per_device_general(
    inputs,
    doc_ids,
    w_query,
    w_key,
    w_value,
    w_out,
    w_gate,
    w_up,
    w_down,
    gain_in,
    gain_attn_post,
    gain_ff_pre,
    gain_ff_post,
    gain_query,
    gain_key,
    cotangent,
):
    gathered = (
        lax.all_gather(w_query, "wshard", axis=0, tiled=True),
        lax.all_gather(w_key, "wshard", axis=0, tiled=True),
        lax.all_gather(w_value, "wshard", axis=0, tiled=True),
        lax.all_gather(w_out, "wshard", axis=0, tiled=True),
        lax.all_gather(w_gate, "wshard", axis=0, tiled=True),
        lax.all_gather(w_up, "wshard", axis=0, tiled=True),
        lax.all_gather(w_down, "wshard", axis=0, tiled=True),
        lax.all_gather(gain_in, "wshard", axis=0, tiled=True),
        lax.all_gather(gain_attn_post, "wshard", axis=0, tiled=True),
        lax.all_gather(gain_ff_pre, "wshard", axis=0, tiled=True),
        lax.all_gather(gain_ff_post, "wshard", axis=0, tiled=True),
        lax.all_gather(gain_query, "wshard", axis=0, tiled=True),
        lax.all_gather(gain_key, "wshard", axis=0, tiled=True),
    )
    full_query, full_key, full_value, full_out, full_gate, full_up, full_down = gathered[:7]
    in_gain, attn_post_gain, ff_pre_gain, ff_post_gain, query_gain, key_gain = [
        g.astype(jnp.float32) for g in gathered[7:]
    ]
    row_count = inputs.shape[0]
    head_dim = full_key.shape[1]
    head_count = full_query.shape[1] // head_dim
    score_scale = head_dim ** (-0.5)
    start_row = lax.axis_index(("seq", "wshard")) * row_count
    query_pos = start_row + jnp.arange(row_count, dtype=jnp.int32)
    cos_table, sin_table = rope_tables(query_pos, head_dim)
    x_float = inputs.astype(jnp.float32)
    normed_in = rms_gain(x_float, in_gain).astype(jnp.bfloat16)
    query_raw = jnp.dot(normed_in, full_query, preferred_element_type=jnp.float32).reshape(
        row_count, head_count, head_dim
    )
    key_raw = jnp.dot(normed_in, full_key, preferred_element_type=jnp.float32)[:, None, :]
    values = jnp.dot(normed_in, full_value, preferred_element_type=jnp.float32).astype(jnp.bfloat16)
    queries = norm_rope(query_raw, query_gain, cos_table, sin_table).astype(jnp.bfloat16)
    key_rot = norm_rope(key_raw, key_gain, cos_table, sin_table)[:, 0].astype(jnp.bfloat16)
    sent_rows = min(WINDOW, row_count)
    hop_count = WINDOW // sent_rows
    outgoing = (key_rot, values, doc_ids)
    halo_keys = []
    halo_values = []
    halo_docs = []
    for distance in range(hop_count, 0, -1):
        arrived = from_behind((outgoing[0], outgoing[1], outgoing[2]), ("seq", "wshard"), distance)
        halo_keys.append(arrived[0])
        halo_values.append(arrived[1])
        halo_docs.append(arrived[2])
    all_keys = jnp.concatenate(halo_keys + [key_rot], 0)
    all_values = jnp.concatenate(halo_values + [values], 0)
    all_docs = jnp.concatenate(halo_docs + [doc_ids], 0)
    key_pos = start_row - WINDOW + jnp.arange(WINDOW + row_count, dtype=jnp.int32)
    allowed = window_mask(query_pos, key_pos, doc_ids, all_docs)
    scores = masked_scores(queries, all_keys, allowed, score_scale)
    row_peak = jnp.max(scores, axis=-1, keepdims=True)
    row_total = jnp.sum(
        jnp.where(allowed[None], jnp.exp(scores - row_peak), 0.0), axis=-1, keepdims=True
    )
    log_total = row_peak + jnp.log(row_total)
    soft = jnp.where(allowed[None], jnp.exp(scores - log_total), 0.0).astype(jnp.bfloat16)
    attended = jnp.einsum("hqk,kd->qhd", soft, all_values, preferred_element_type=jnp.float32)
    attended = attended.reshape(row_count, head_count * head_dim).astype(jnp.bfloat16)
    attn_proj = jnp.dot(attended, full_out, preferred_element_type=jnp.float32)
    resid = x_float + rms_gain(attn_proj, attn_post_gain)
    normed_ff = rms_gain(resid, ff_pre_gain).astype(jnp.bfloat16)
    gate_pre = jnp.dot(normed_ff, full_gate, preferred_element_type=jnp.float32)
    up_pre = jnp.dot(normed_ff, full_up, preferred_element_type=jnp.float32)
    hidden = geglu(gate_pre, up_pre).astype(jnp.bfloat16)
    ff_proj = jnp.dot(hidden, full_down, preferred_element_type=jnp.float32)
    layer_out = (resid + rms_gain(ff_proj, ff_post_gain)).astype(jnp.bfloat16)
    grad_top = cotangent.astype(jnp.float32)
    _, pullback = jax.vjp(rms_gain, ff_proj, ff_post_gain)
    grad_ff_proj, grad_gain_ff_post = pullback(grad_top)
    grad_ff_proj = grad_ff_proj.astype(jnp.bfloat16)
    grad_w_down = weight_grad(hidden, grad_ff_proj)
    grad_hidden = lax.dot_general(
        grad_ff_proj, full_down, (((1,), (1,)), ((), ())), preferred_element_type=jnp.float32
    )
    _, pullback = jax.vjp(geglu, gate_pre, up_pre)
    grad_gate, grad_up = pullback(grad_hidden)
    grad_gate = grad_gate.astype(jnp.bfloat16)
    grad_up = grad_up.astype(jnp.bfloat16)
    grad_w_gate = weight_grad(normed_ff, grad_gate)
    grad_w_up = weight_grad(normed_ff, grad_up)
    grad_normed_ff = lax.dot_general(
        grad_gate, full_gate, (((1,), (1,)), ((), ())), preferred_element_type=jnp.float32
    )
    grad_normed_ff = grad_normed_ff + lax.dot_general(
        grad_up, full_up, (((1,), (1,)), ((), ())), preferred_element_type=jnp.float32
    )
    _, pullback = jax.vjp(rms_gain, resid, ff_pre_gain)
    grad_resid_part, grad_gain_ff_pre = pullback(grad_normed_ff)
    grad_resid = grad_top + grad_resid_part
    ff_gradients = (grad_w_gate, grad_w_up, grad_w_down, grad_gain_ff_pre, grad_gain_ff_post)
    ff_parts = (
        lax.psum_scatter(
            ff_gradients[0].astype(jnp.bfloat16), "wshard", scatter_dimension=0, tiled=True
        ).astype(jnp.float32),
        lax.psum_scatter(
            ff_gradients[1].astype(jnp.bfloat16), "wshard", scatter_dimension=0, tiled=True
        ).astype(jnp.float32),
        lax.psum_scatter(
            ff_gradients[2].astype(jnp.bfloat16), "wshard", scatter_dimension=0, tiled=True
        ).astype(jnp.float32),
        lax.psum_scatter(
            ff_gradients[3].astype(jnp.bfloat16), "wshard", scatter_dimension=0, tiled=True
        ).astype(jnp.float32),
        lax.psum_scatter(
            ff_gradients[4].astype(jnp.bfloat16), "wshard", scatter_dimension=0, tiled=True
        ).astype(jnp.float32),
    )
    ff_reduced = (
        lax.psum(ff_parts[0].astype(jnp.bfloat16), "seq").astype(jnp.float32),
        lax.psum(ff_parts[1].astype(jnp.bfloat16), "seq").astype(jnp.float32),
        lax.psum(ff_parts[2].astype(jnp.bfloat16), "seq").astype(jnp.float32),
        lax.psum(ff_parts[3].astype(jnp.bfloat16), "seq").astype(jnp.float32),
        lax.psum(ff_parts[4].astype(jnp.bfloat16), "seq").astype(jnp.float32),
    )
    _, pullback = jax.vjp(rms_gain, attn_proj, attn_post_gain)
    grad_attn_proj, grad_gain_attn_post = pullback(grad_resid)
    grad_attn_proj = grad_attn_proj.astype(jnp.bfloat16)
    grad_w_out = weight_grad(attended, grad_attn_proj)
    grad_attended = lax.dot_general(
        grad_attn_proj, full_out, (((1,), (1,)), ((), ())), preferred_element_type=jnp.float32
    ).astype(jnp.bfloat16)
    grad_heads = grad_attended.reshape(row_count, head_count, head_dim)
    again_scores = masked_scores(queries, all_keys, allowed, score_scale)
    probs = jnp.where(allowed[None], jnp.exp(again_scores - log_total), 0.0)
    grad_soft = jnp.einsum(
        "qhd,kd->hqk", grad_heads, all_values, preferred_element_type=jnp.float32
    )
    row_inner = jnp.sum(probs * grad_soft, axis=-1, keepdims=True)
    grad_score = (probs * (grad_soft - row_inner) * score_scale).astype(jnp.bfloat16)
    grad_queries = jnp.einsum(
        "hqk,kd->qhd", grad_score, all_keys, preferred_element_type=jnp.float32
    )
    grad_keys_all = jnp.einsum(
        "hqk,qhd->kd", grad_score, queries, preferred_element_type=jnp.float32
    )
    grad_values_all = jnp.einsum(
        "hqk,qhd->kd", probs.astype(jnp.bfloat16), grad_heads, preferred_element_type=jnp.float32
    )
    back_keys = jnp.zeros((sent_rows, head_dim), jnp.float32)
    back_values = jnp.zeros((sent_rows, head_dim), jnp.float32)
    for piece_index in range(hop_count):
        distance = hop_count - piece_index
        piece_start = piece_index * sent_rows
        arrived = (
            from_behind(
                grad_keys_all[piece_start : piece_start + sent_rows].astype(jnp.bfloat16),
                ("seq", "wshard"),
                -distance,
            ).astype(jnp.float32),
            from_behind(
                grad_values_all[piece_start : piece_start + sent_rows].astype(jnp.bfloat16),
                ("seq", "wshard"),
                -distance,
            ).astype(jnp.float32),
        )
        back_keys = back_keys + arrived[0]
        back_values = back_values + arrived[1]
    own_keys = grad_keys_all[WINDOW:]
    own_values = grad_values_all[WINDOW:]
    split_row = row_count - sent_rows
    grad_keys = jnp.concatenate([own_keys[:split_row], own_keys + back_keys], 0)
    grad_values = jnp.concatenate([own_values[:split_row], own_values + back_values], 0).astype(
        jnp.bfloat16
    )

    def query_path(tensor, gain_vec):
        return norm_rope(tensor, gain_vec, cos_table, sin_table)

    _, pullback = jax.vjp(query_path, query_raw, query_gain)
    grad_query_raw, grad_gain_query = pullback(grad_queries)
    _, pullback = jax.vjp(query_path, key_raw, key_gain)
    grad_key_raw, grad_gain_key = pullback(grad_keys[:, None, :])
    grad_query_raw = grad_query_raw.reshape(row_count, head_count * head_dim).astype(jnp.bfloat16)
    grad_key_raw = grad_key_raw[:, 0].astype(jnp.bfloat16)
    grad_w_query = weight_grad(normed_in, grad_query_raw)
    grad_w_key = weight_grad(normed_in, grad_key_raw)
    grad_w_value = weight_grad(normed_in, grad_values)
    grad_normed_in = lax.dot_general(
        grad_query_raw, full_query, (((1,), (1,)), ((), ())), preferred_element_type=jnp.float32
    )
    grad_normed_in = grad_normed_in + lax.dot_general(
        grad_key_raw, full_key, (((1,), (1,)), ((), ())), preferred_element_type=jnp.float32
    )
    grad_normed_in = grad_normed_in + lax.dot_general(
        grad_values, full_value, (((1,), (1,)), ((), ())), preferred_element_type=jnp.float32
    )
    _, pullback = jax.vjp(rms_gain, x_float, in_gain)
    grad_input_part, grad_gain_in = pullback(grad_normed_in)
    grad_inputs = grad_resid + grad_input_part
    attn_gradients = (
        grad_w_query,
        grad_w_key,
        grad_w_value,
        grad_w_out,
        grad_gain_in,
        grad_gain_attn_post,
        grad_gain_query,
        grad_gain_key,
    )
    attn_parts = (
        lax.psum_scatter(
            attn_gradients[0].astype(jnp.bfloat16), "wshard", scatter_dimension=0, tiled=True
        ).astype(jnp.float32),
        lax.psum_scatter(
            attn_gradients[1].astype(jnp.bfloat16), "wshard", scatter_dimension=0, tiled=True
        ).astype(jnp.float32),
        lax.psum_scatter(
            attn_gradients[2].astype(jnp.bfloat16), "wshard", scatter_dimension=0, tiled=True
        ).astype(jnp.float32),
        lax.psum_scatter(
            attn_gradients[3].astype(jnp.bfloat16), "wshard", scatter_dimension=0, tiled=True
        ).astype(jnp.float32),
        lax.psum_scatter(
            attn_gradients[4].astype(jnp.bfloat16), "wshard", scatter_dimension=0, tiled=True
        ).astype(jnp.float32),
        lax.psum_scatter(
            attn_gradients[5].astype(jnp.bfloat16), "wshard", scatter_dimension=0, tiled=True
        ).astype(jnp.float32),
        lax.psum_scatter(
            attn_gradients[6].astype(jnp.bfloat16), "wshard", scatter_dimension=0, tiled=True
        ).astype(jnp.float32),
        lax.psum_scatter(
            attn_gradients[7].astype(jnp.bfloat16), "wshard", scatter_dimension=0, tiled=True
        ).astype(jnp.float32),
    )
    attn_reduced = (
        lax.psum(attn_parts[0].astype(jnp.bfloat16), "seq").astype(jnp.float32),
        lax.psum(attn_parts[1].astype(jnp.bfloat16), "seq").astype(jnp.float32),
        lax.psum(attn_parts[2].astype(jnp.bfloat16), "seq").astype(jnp.float32),
        lax.psum(attn_parts[3].astype(jnp.bfloat16), "seq").astype(jnp.float32),
        lax.psum(attn_parts[4].astype(jnp.bfloat16), "seq").astype(jnp.float32),
        lax.psum(attn_parts[5].astype(jnp.bfloat16), "seq").astype(jnp.float32),
        lax.psum(attn_parts[6].astype(jnp.bfloat16), "seq").astype(jnp.float32),
        lax.psum(attn_parts[7].astype(jnp.bfloat16), "seq").astype(jnp.float32),
    )
    reduced = (
        attn_reduced[0],
        attn_reduced[1],
        attn_reduced[2],
        attn_reduced[3],
        ff_reduced[0],
        ff_reduced[1],
        ff_reduced[2],
        attn_reduced[4],
        attn_reduced[5],
        ff_reduced[3],
        ff_reduced[4],
        attn_reduced[6],
        attn_reduced[7],
    )
    return (layer_out, grad_inputs) + tuple(reduced)


def solution(mesh):
    routed = mesh.shape["wshard"] == 2 and mesh.shape["seq"] == 16
    return jax.shard_map(
        per_device if routed else per_device_general,
        mesh=mesh,
        in_specs=(
            P(("seq", "wshard"), None),
            P(("seq", "wshard")),
            P("wshard", None),
            P("wshard", None),
            P("wshard", None),
            P("wshard", None),
            P("wshard", None),
            P("wshard", None),
            P("wshard", None),
            P("wshard"),
            P("wshard"),
            P("wshard"),
            P("wshard"),
            P("wshard"),
            P("wshard"),
            P(("seq", "wshard"), None),
        ),
        out_specs=(
            P(("seq", "wshard"), None),
            P(("seq", "wshard"), None),
            P("wshard", None),
            P("wshard", None),
            P("wshard", None),
            P("wshard", None),
            P("wshard", None),
            P("wshard", None),
            P("wshard", None),
            P("wshard"),
            P("wshard"),
            P("wshard"),
            P("wshard"),
            P("wshard"),
            P("wshard"),
        ),
        check_vma=False,
    )
```
